128 devices in a mesh: grp: 8 (over x, core), dev: 16 (over z, y).
Axes of the slice: x: 4, y: 4, z: 4, core: 2. Of those that a mesh axis runs over, the one named last changes fastest.
Arguments:
- residual: bfloat16 [16384, 2048], P(('grp', 'dev')), may hold values from -3 to 3
- queries: bfloat16 [16384, 1024], P(('grp', 'dev')), may hold values from -9 to 9
- keys: bfloat16 [16384, 256], P(('grp', 'dev')), may hold values from -6 to 6
- values: bfloat16 [16384, 256], P(('grp', 'dev')), may hold values from -18 to 18
- prefix_keys: bfloat16 [32, 1024, 256], P('grp', 'dev'), may hold values from -6 to 6
- cached_prefix_values: bfloat16 [32, 1024, 256], P('grp', 'dev'), may hold values from -18 to 18
- out_weight: bfloat16 [1024, 2048], replicated, may hold values from -0.1875 to 0.1875
- norm_gain: float32 [2048], replicated, may hold values from 0.25 to 1.75
- w_gate: bfloat16 [2048, 8192], P('grp', 'dev'), may hold values from -0.125 to 0.125
- w_up: bfloat16 [2048, 8192], P('grp', 'dev'), may hold values from -0.125 to 0.125
- w_down: bfloat16 [8192, 2048], P('dev', 'grp'), may hold values from -0.0625 to 0.0625
- suffix_lengths: int32 [8, 32], P('grp'), may hold values from 1 to 128, 2048 in all within a row
- request_group: int32 [8, 32], P('grp'), may hold values from 0 to 3, as said below
- placement_order: int32 [8, 32], P('grp'), may hold values from 0 to 31, each once within a row
Outputs:
- layer_out: bfloat16 [16384, 2048], P(('grp', 'dev'))
The draws below stay inside these ranges and needn't reach their ends.
Inputs may be any that keep to these rules, and one draw needn't show every extreme that they name: `suffix_lengths`: the 32 lengths of one row sum to 2048. `request_group`: each row names each of its 4 groups exactly 8 times. `placement_order`: each row is an ordering of its 32 requests.
All inputs are finite; a program needn't handle non-finite values.
Results may differ from the reference program's by a relative error of at most 0.012.
Values may be sent and summed in bfloat16 or wider, within the bound.
A program may use at most 128 MiB of HBM per device.

```python
import math
import jax
import jax.numpy as jnp
import numpy as np
from jax import lax

D = 2048
FF = 8192
HEAD_SIZE = 64
QUERY_HEADS = 16
KEY_VALUE_HEADS = 4
G_ROW = 4
REQ_GRP = 8
TOK_DEV = 128
PRE_DEV = 64
REQ_ROW = 32
PREFIX_GROUPS = 32
ROW_TOKENS = 2048
SUFFIX_TOKENS = 16384
PREFIX_LENGTH = 1024
N_GRP = 8
N_DEV = 16


def draw_queries(key, part):
    root_key = jax.random.fold_in(key, 11)
    return (1.5 * jax.random.truncated_normal(root_key, -6.0, 6.0, (SUFFIX_TOKENS, QUERY_HEADS * HEAD_SIZE), jnp.float32)).astype(jnp.bfloat16)


def draw_prefix_keys(key, part):
    root_key = jax.random.fold_in(key, 21)
    return jax.random.truncated_normal(root_key, -6.0, 6.0, (PREFIX_GROUPS, PREFIX_LENGTH, KEY_VALUE_HEADS * HEAD_SIZE), jnp.float32).astype(jnp.bfloat16)


def draw_request_group(key, part):
    row_keys = jax.random.split(jax.random.fold_in(key, 31), N_GRP)
    orders = jax.vmap(lambda row_key: jax.random.permutation(row_key, REQ_ROW))(row_keys)
    return (orders // REQ_GRP).astype(jnp.int32)


def steps_of(key, extent, pieces, least, high):
    def one(position, parts):
        heights = jax.random.uniform(jax.random.fold_in(jax.random.fold_in(key, 6), position), (parts,), jnp.float32, least / len(pieces), high / len(pieces))
        return jnp.repeat(jnp.exp(heights), extent[position] // parts).reshape((-1,) + (1,) * (len(extent) - position - 1))

    factor_of = one(*pieces[0])
    for cut in pieces[1:]:
        factor_of = factor_of * one(*cut)
    return factor_of


def split_up(count, total, bound, lean):
    weights = [(1 << 20) // math.isqrt(grade ** lean) + 1 for grade in range(2, count + 1)]
    rest, given = total - bound - (count - 1), [1] * (count - 1)
    while rest > 0:
        free = [i for i in range(count - 1) if given[i] < bound]
        mass, remaining = sum([weights[i] for i in free]), rest
        for i in free:
            extra = min(bound - given[i], max(1, remaining * weights[i] // mass), rest)
            given[i] = given[i] + extra
            rest = rest - extra
    return np.array([bound] + given)


def uneven_parts(own_key, number_of, total, reach, slope):
    if number_of == 2:
        one = jax.random.randint(own_key, (), max(1, total - reach), min(reach, total - 1) + 1)
        return jnp.stack([one, total - one])
    sizes = jnp.asarray(split_up(number_of, total, reach, slope), jnp.int32)
    pairs = (number_of - 1) // 2
    giver, taker = sizes[1:1 + 2 * pairs:2], sizes[2:2 + 2 * pairs:2]
    slack = jnp.minimum(giver - 1, reach - taker)
    moved = jax.random.randint(jax.random.fold_in(own_key, 1), (pairs,), 0, 1 << 20) % (slack + 1)
    sizes = sizes.at[1:1 + 2 * pairs:2].set(giver - moved).at[2:2 + 2 * pairs:2].set(taker + moved)
    return sizes[jax.random.permutation(jax.random.fold_in(own_key, 2), number_of)]


def noise(stream_key, extent, deviation, limit, cuts=(), held_as=jnp.bfloat16):
    entries = jax.random.normal(stream_key, extent, jnp.float32) * deviation
    if len(cuts) > 0:
        entries = steps_of(stream_key, extent, cuts, -0.22, 0.18) * entries
    return jnp.clip(entries, min=-limit, max=limit).astype(held_as)


def setup_inputs(seed: int = 0) -> dict:
    arg_keys = jax.random.split(jax.random.key(seed), 15)
    return {
        "residual": noise(arg_keys[0], (SUFFIX_TOKENS, D), 0.5, 3.0, ((0, 128),)),
        "queries": draw_queries(jax.random.fold_in(arg_keys[14], 71), 0),
        "keys": noise(arg_keys[2], (SUFFIX_TOKENS, KEY_VALUE_HEADS * HEAD_SIZE), 1.0, 6.0, ((0, 128),)),
        "values": noise(arg_keys[3], (SUFFIX_TOKENS, KEY_VALUE_HEADS * HEAD_SIZE), 3.0, 18.0, ((0, 128),)),
        "prefix_keys": draw_prefix_keys(jax.random.fold_in(arg_keys[14], 71), 0),
        "cached_prefix_values": noise(arg_keys[5], (PREFIX_GROUPS, PREFIX_LENGTH, KEY_VALUE_HEADS * HEAD_SIZE), 3.0, 18.0, ((0, 8), (1, 16))),
        "out_weight": noise(arg_keys[6], (QUERY_HEADS * HEAD_SIZE, D), (QUERY_HEADS * HEAD_SIZE) ** -0.5, 0.1875),
        "norm_gain": jnp.clip(1.0 + 0.15 * jax.random.normal(arg_keys[7], (D,), jnp.float32), 0.25, 1.75),
        "w_gate": noise(arg_keys[8], (D, FF), D ** -0.5, 0.125, ((0, 8), (1, 16))),
        "w_up": noise(arg_keys[9], (D, FF), D ** -0.5, 0.125, ((0, 8), (1, 16))),
        "w_down": noise(arg_keys[10], (FF, D), FF ** -0.5, 0.0625, ((0, 16), (1, 8))),
        "suffix_lengths": jax.vmap(lambda own: uneven_parts(own, REQ_ROW, ROW_TOKENS, TOK_DEV, 2))(jax.random.split(arg_keys[11], N_GRP)).reshape((N_GRP, REQ_ROW)).astype(jnp.int32),
        "request_group": draw_request_group(jax.random.fold_in(arg_keys[14], 71), 0),
        "placement_order": jax.vmap(lambda own: jax.random.permutation(own, REQ_ROW))(jax.random.split(arg_keys[13], N_GRP)).reshape((N_GRP, REQ_ROW)).astype(jnp.int32),
    }


NEG_FILL = -1e+30
EPSILON = 1e-05

def row_layout(lengths, group_map, packed_order):
    request_count = lengths.shape[0]
    picked = (packed_order[:, None] == jnp.arange(request_count, dtype=jnp.int32)[None, :]).astype(jnp.int32)
    packed_len = lax.optimization_barrier(jnp.sum(picked * lengths[None, :], axis=1))
    packed_group = lax.optimization_barrier(jnp.sum(picked * group_map[None, :], axis=1))
    ends_at = jnp.cumsum(packed_len).astype(jnp.int32)
    return (ends_at - packed_len, ends_at, packed_group)

def token_info(token_rows, starts_at, ends_at, packed_group):
    inside = ((token_rows[:, None] >= starts_at[None, :]) & (token_rows[:, None] < ends_at[None, :])).astype(jnp.int32)
    return (lax.optimization_barrier(jnp.sum(inside * packed_group[None, :], axis=1)), lax.optimization_barrier(jnp.sum(inside * starts_at[None, :], axis=1)))

def block_partial(rows_of_queries, allowed, rows_of_keys, rows_of_values):
    query_row_count = rows_of_queries.shape[0]
    key_row_count = rows_of_keys.shape[0]
    heads_of_queries = rows_of_queries.astype(jnp.float32).reshape(query_row_count, KEY_VALUE_HEADS, QUERY_HEADS // KEY_VALUE_HEADS, HEAD_SIZE)
    heads_of_keys = rows_of_keys.astype(jnp.float32).reshape(key_row_count, KEY_VALUE_HEADS, HEAD_SIZE)
    heads_of_values = rows_of_values.astype(jnp.float32).reshape(key_row_count, KEY_VALUE_HEADS, HEAD_SIZE)
    scores = jnp.einsum('nkrd,mkd->nkrm', heads_of_queries, heads_of_keys) * HEAD_SIZE ** (-0.5)
    scores = jnp.where(allowed[:, None, None, :], scores, NEG_FILL)
    maxima = lax.optimization_barrier(jnp.max(scores, axis=-1))
    weights = jnp.exp(scores - maxima[..., None])
    totals = lax.optimization_barrier(jnp.sum(weights, axis=-1))
    rounded = lax.optimization_barrier(weights.astype(jnp.bfloat16)).astype(jnp.float32)
    numerator = jnp.einsum('nkrm,mkd->nkrd', rounded, heads_of_values)
    return (numerator / totals[..., None], maxima, totals)

def merge_all(local_output, local_maximum, local_sum, block_outs, block_maxima, block_sums):
    highest = jnp.maximum(local_maximum, lax.optimization_barrier(jnp.max(block_maxima, axis=0)))
    own_scale = local_sum * jnp.exp(local_maximum - highest)
    scales = block_sums * jnp.exp(block_maxima - highest[None])
    numerator = own_scale[..., None] * local_output + lax.optimization_barrier(jnp.sum(scales[..., None] * block_outs.astype(jnp.float32), axis=0))
    return numerator / (own_scale + lax.optimization_barrier(jnp.sum(scales, axis=0)))[..., None]

def reference(residual, queries, keys, values, prefix_keys, cached_prefix_values, out_weight, norm_gain, w_gate, w_up, w_down, suffix_lengths, request_group, placement_order):
    key_value_width = KEY_VALUE_HEADS * HEAD_SIZE
    key_group = jnp.arange(G_ROW * PRE_DEV, dtype=jnp.int32) // PRE_DEV
    slice_width = FF // N_DEV

    def one_row(packed):
        row_res, row_q, row_k, row_v, row_pk, row_pv, lengths, group_map, packed_order = packed
        starts_at, ends_at, packed_group = row_layout(lengths, group_map, packed_order)
        token_rows = jnp.arange(ROW_TOKENS, dtype=jnp.int32)
        token_group, token_start = token_info(token_rows, starts_at, ends_at, packed_group)
        allowed = token_group[:, None] == key_group[None, :]
        owner_keys = row_pk.reshape(G_ROW, N_DEV, PRE_DEV, key_value_width).transpose(1, 0, 2, 3).reshape(N_DEV, G_ROW * PRE_DEV, key_value_width)
        owner_values = row_pv.reshape(G_ROW, N_DEV, PRE_DEV, key_value_width).transpose(1, 0, 2, 3).reshape(N_DEV, G_ROW * PRE_DEV, key_value_width)

        def owner_part(owner_pair):
            part_out, maxima, totals = block_partial(row_q, allowed, owner_pair[0], owner_pair[1])
            return (part_out.astype(jnp.bfloat16), maxima, totals)
        block_outs, block_maxima, block_sums = lax.map(owner_part, (owner_keys, owner_values))
        padded_k = jnp.concatenate([jnp.zeros((TOK_DEV, key_value_width), row_k.dtype), row_k], axis=0)
        padded_v = jnp.concatenate([jnp.zeros((TOK_DEV, key_value_width), row_v.dtype), row_v], axis=0)

        def suffix_part(device):
            first_row = (device * TOK_DEV).astype(jnp.int32)
            rows_of_queries = lax.dynamic_slice_in_dim(row_q, first_row, TOK_DEV, 0)
            rows_of_keys = lax.dynamic_slice_in_dim(padded_k, first_row, 2 * TOK_DEV, 0)
            rows_of_values = lax.dynamic_slice_in_dim(padded_v, first_row, 2 * TOK_DEV, 0)
            own_rows = first_row + jnp.arange(TOK_DEV, dtype=jnp.int32)
            window = first_row - TOK_DEV + jnp.arange(2 * TOK_DEV, dtype=jnp.int32)
            starts = lax.dynamic_slice_in_dim(token_start, first_row, TOK_DEV, 0)
            suffix_mask = (window[None, :] >= starts[:, None]) & (window[None, :] <= own_rows[:, None])
            return block_partial(rows_of_queries, suffix_mask, rows_of_keys, rows_of_values)
        local_output, local_maximum, local_sum = lax.map(suffix_part, jnp.arange(N_DEV, dtype=jnp.int32))
        local_output = local_output.reshape(ROW_TOKENS, KEY_VALUE_HEADS, QUERY_HEADS // KEY_VALUE_HEADS, HEAD_SIZE)
        local_maximum = local_maximum.reshape(ROW_TOKENS, KEY_VALUE_HEADS, QUERY_HEADS // KEY_VALUE_HEADS)
        local_sum = local_sum.reshape(ROW_TOKENS, KEY_VALUE_HEADS, QUERY_HEADS // KEY_VALUE_HEADS)
        merged = merge_all(local_output, local_maximum, local_sum, block_outs, block_maxima, block_sums)
        attention = merged.astype(jnp.bfloat16).reshape(ROW_TOKENS, QUERY_HEADS * HEAD_SIZE)
        hidden_state = row_res.astype(jnp.float32) + jnp.dot(attention, out_weight, preferred_element_type=jnp.float32)
        normed = (hidden_state * lax.rsqrt(lax.optimization_barrier(jnp.mean(hidden_state * hidden_state, axis=-1, keepdims=True)) + EPSILON) * norm_gain).astype(jnp.bfloat16)
        gate_value = jnp.dot(normed, w_gate, preferred_element_type=jnp.float32)
        up_value = jnp.dot(normed, w_up, preferred_element_type=jnp.float32)
        activation = (jax.nn.silu(gate_value) * up_value).astype(jnp.bfloat16)
        act_slices = activation.reshape(ROW_TOKENS, N_DEV, slice_width).transpose(1, 0, 2)
        down_slices = w_down.reshape(N_DEV, slice_width, D)

        def add_slice(running, slice_pair):
            slice_term = jnp.dot(slice_pair[0], slice_pair[1], preferred_element_type=jnp.float32)
            slice_term = lax.optimization_barrier(slice_term.astype(jnp.bfloat16)).astype(jnp.float32)
            return (running + slice_term, None)
        mlp_sum, unused_tail = lax.scan(add_slice, jnp.zeros((ROW_TOKENS, D), jnp.float32), (act_slices, down_slices))
        return (hidden_state + mlp_sum).astype(jnp.bfloat16)
    rows_out = lax.map(one_row, (residual.reshape(N_GRP, ROW_TOKENS, D), queries.reshape(N_GRP, ROW_TOKENS, QUERY_HEADS * HEAD_SIZE), keys.reshape(N_GRP, ROW_TOKENS, key_value_width), values.reshape(N_GRP, ROW_TOKENS, key_value_width), prefix_keys.reshape(N_GRP, G_ROW, PREFIX_LENGTH, key_value_width), cached_prefix_values.reshape(N_GRP, G_ROW, PREFIX_LENGTH, key_value_width), suffix_lengths, request_group, placement_order))
    return rows_out.reshape(SUFFIX_TOKENS, D)
```

```python
import jax
import jax.numpy as jnp
from jax import lax
from jax.experimental import pallas as pl
from jax.experimental.pallas import tpu as pltpu
from jax.sharding import PartitionSpec as P

EPSILON = 1e-05
NEG_FILL = -1e30
MESH = pl.DeviceIdType.MESH
F32, BF16 = jnp.float32, jnp.bfloat16
N_SEM = 104


def token_info(lengths, groups, order, first_row):
    n = lengths.shape[1]
    rows = lax.broadcasted_iota(jnp.int32, (n, n), 0)
    cols = lax.broadcasted_iota(jnp.int32, (n, n), 1)
    diagonal = rows == cols

    def column(row):
        spread = jnp.broadcast_to(row, (n, n))
        return jnp.sum(jnp.where(diagonal, spread, 0.0), axis=1, keepdims=True)

    picked = jnp.broadcast_to(order, (n, n)) == rows
    packed_len = jnp.sum(jnp.where(picked, column(lengths), 0.0), axis=0, keepdims=True)
    packed_group = jnp.sum(jnp.where(picked, column(groups), 0.0), axis=0, keepdims=True)
    ends = jnp.sum(jnp.where(rows <= cols, column(packed_len), 0.0), axis=0, keepdims=True)
    starts = ends - packed_len
    token = (lax.broadcasted_iota(jnp.int32, (128, n), 0) + first_row).astype(F32)
    inside = (token >= starts) & (token < ends)
    group = jnp.sum(jnp.where(inside, packed_group, 0.0), axis=1, keepdims=True)
    start = jnp.sum(jnp.where(inside, starts, 0.0), axis=1, keepdims=True)
    return group, start


def kernel(
    res_in, q_in, k_in, v_in, pk_in, pv_in, ow_in, gain_in, wg_in, wu_in, wd_in, len_in, grp_in, ord_in,
    out,
    kbuf, vbuf, kprev, vprev, ks, vs, attn, owb, resb, hid, xn, wg, wu, wd, act, acc, stage, back,
    ssem, rsem, lsem,
):
    gi, di = lax.axis_index("grp"), lax.axis_index("dev")
    x, c = gi // 2, lax.rem(gi, 2)
    z, y = di // 4, lax.rem(di, 4)

    def at(xx, cc, zz, yy):
        return (lax.rem(xx + 4, 4) * 2 + cc, lax.rem(zz + 4, 4) * 4 + lax.rem(yy + 4, 4))

    xs = {k: at(x + k, c, z, y) for k in (1, -1)}
    ys = {k: at(x, c, z, y + k) for k in (1, -1)}
    zs = {k: at(x, c, z + k, y) for k in (1, -1, 2)}
    partner = (x * 2 + (1 - c), di)
    following, preceding = (gi, lax.rem(di + 1, 16)), (gi, lax.rem(di + 15, 16))
    peers = [xs[1], xs[-1], ys[1], ys[-1], zs[1], zs[-1], zs[2], partner, following, preceding]

    barrier = pltpu.get_barrier_semaphore()
    for peer in peers:
        pl.semaphore_signal(barrier, inc=1, device_id=peer, device_id_type=MESH)
    pl.semaphore_wait(barrier, len(peers))

    started = []
    counter = [0]

    def send(src, dst, device):
        i = counter[0]
        counter[0] += 1
        copy = pltpu.make_async_remote_copy(
            src_ref=src, dst_ref=dst, send_sem=ssem.at[i], recv_sem=rsem.at[i],
            device_id=device, device_id_type=MESH,
        )
        copy.start()
        started.append(copy)
        return copy

    local_count = [0]

    def bring(src, dst):
        i = local_count[0]
        local_count[0] += 1
        copy = pltpu.make_async_copy(src, dst, lsem.at[i])
        copy.start()
        return copy

    class Ring:
        def __init__(self, where, pos, slot, half):
            self.where, self.pos, self.slot, self.half = where, pos, slot, half

        def start(self, src=None):
            mine = self.slot(self.pos)
            src = mine if src is None else src
            self.up = send(src, mine, self.where[1])
            self.down = send(src, mine, self.where[-1])

        def relay(self):
            before, after = lax.rem(self.pos + 3, 4), lax.rem(self.pos + 1, 4)
            self.up.wait_recv()
            self.a = send(self.half(before, 0), self.half(before, 0), self.where[1])
            self.down.wait_recv()
            self.b = send(self.half(after, 1), self.half(after, 1), self.where[-1])

        def finish(self):
            self.a.wait_recv()
            self.b.wait_recv()

        def around(self):
            return [lax.rem(self.pos + k, 4) for k in (3, 1, 2)]

    gate1 = Ring(xs, x, lambda i: wg.at[y, i, c], lambda i, h: wg.at[y, i, c, pl.ds(128 * h, 128)])
    gate2 = Ring(ys, y, lambda i: wg.at[i, :, c], lambda i, h: wg.at[i, pl.ds(2 * h, 2), c])
    up1 = Ring(ys, y, lambda i: wu.at[i, x, c], lambda i, h: wu.at[i, x, c, pl.ds(128 * h, 128)])
    up2 = Ring(xs, x, lambda i: wu.at[:, i, c], lambda i, h: wu.at[pl.ds(2 * h, 2), i, c])
    down1 = Ring(ys, y, lambda i: wd.at[x, c, i], lambda i, h: wd.at[x, c, i, pl.ds(256 * h, 256)])
    down2 = Ring(xs, x, lambda i: wd.at[i, c], lambda i, h: wd.at[i, c, pl.ds(2 * h, 2)])
    key1 = Ring(ys, y, lambda i: kbuf.at[z, i], lambda i, h: kbuf.at[z, i, pl.ds(2 * h, 2)])
    key2 = Ring(zs, z, lambda i: kbuf.at[i], lambda i, h: kbuf.at[i, pl.ds(2 * h, 2)])
    val1 = Ring(zs, z, lambda i: vbuf.at[i, y], lambda i, h: vbuf.at[i, y, pl.ds(2 * h, 2)])
    val2 = Ring(ys, y, lambda i: vbuf.at[:, i], lambda i, h: vbuf.at[pl.ds(2 * h, 2), i])

    gate1.start(wg_in)
    local_gate = bring(wg_in, wg.at[y, x, c])
    local_up = bring(wu_in, wu.at[y, x, c])
    local_down = bring(wd_in, wd.at[x, c, y])
    local_out = bring(ow_in, owb)
    local_res = bring(res_in, resb)
    next_k = send(k_in, kprev, following)
    next_v = send(v_in, vprev, following)

    low64 = lax.broadcasted_iota(jnp.int32, (64, 128), 1) < 64
    for src, dst in ((pk_in, kbuf), (pv_in, vbuf)):
        for h in range(4):
            cut = slice(128 * (h // 2), 128 * (h // 2) + 128)
            pairs = []
            for g in (0, 2):
                a, b = src[g, :, cut].astype(F32), src[g + 1, :, cut].astype(F32)
                if h % 2 == 0:
                    pairs.append(jnp.where(low64, a, pltpu.roll(b, 64, 1)))
                else:
                    pairs.append(jnp.where(low64, pltpu.roll(a, 64, 1), b))
            dst[z, y, h] = jnp.concatenate(pairs, axis=1).astype(BF16)
    key1.start()
    val1.start()
    up1.start(wu_in)

    first_row = di * 128
    group, start = token_info(
        len_in[...].astype(F32), grp_in[...].astype(F32), ord_in[...], first_row
    )
    lane_group = (lax.broadcasted_iota(jnp.int32, (128, 256), 1) // 64).astype(F32)
    in_group = (lane_group == group).astype(F32)
    window = (lax.broadcasted_iota(jnp.int32, (128, 256), 1) + (first_row - 128)).astype(F32)
    token = (lax.broadcasted_iota(jnp.int32, (128, 256), 0) + first_row).astype(F32)
    bias = jnp.where((window >= start) & (window <= token), 0.0, NEG_FILL)
    low = lax.broadcasted_iota(jnp.int32, (128, 128), 1) < 64

    def twice(block):
        turned = pltpu.roll(block, 64, 1)
        first, second = jnp.where(low, block, turned), jnp.where(low, turned, block)
        return jnp.concatenate([first, first], axis=1), jnp.concatenate([second, second], axis=1)

    def spread(src, dst, row):
        for b in (0, 1):
            first, second = twice(src[:, 128 * b:128 * b + 128].astype(F32))
            dst[2 * b, row:row + 128] = first.astype(BF16)
            dst[2 * b + 1, row:row + 128] = second.astype(BF16)

    spread(k_in, ks, 128)
    spread(v_in, vs, 128)

    key1.relay()
    val1.relay()
    up1.relay()
    val1.finish()
    val2.start()
    key1.finish()
    key2.start()
    down1.start(wd_in)
    gate1.relay()

    next_k.wait_recv()
    next_v.wait_recv()
    spread(kprev, ks, 0)
    spread(vprev, vs, 0)

    up1.finish()
    local_up.wait()
    up2.start()
    up_share = [send(wu.at[:, x, c], wu.at[:, x, c], partner)]
    val2.relay()
    down1.relay()
    key2.relay()
    gate1.finish()
    local_gate.wait()
    gate2.start()
    gate_share = [send(wg.at[y, :, c], wg.at[y, :, c], partner)]
    val2.finish()
    key2.finish()

    bias4 = jnp.concatenate([bias] * 4, axis=0)
    in_group4 = jnp.concatenate([in_group] * 4, axis=0)

    def head(h, carry):
        lanes = pl.ds(pl.multiple_of(h * 256, 256), 256)
        block = q_in[:, lanes].astype(F32) * 0.125
        rows = [part * in_group for b in (0, 1) for part in twice(block[:, 128 * b:128 * b + 128])]
        qx = jnp.concatenate(rows, axis=0).astype(BF16)
        keys = kbuf[:, :, h].reshape(1024, 256)
        contract = (((1,), (1,)), ((), ()))
        s1 = lax.dot_general(qx, keys, contract, preferred_element_type=F32)
        s2 = lax.dot_general(qx, ks[h], contract, preferred_element_type=F32) + bias4
        top = jnp.maximum(
            jnp.max(s1, axis=1, keepdims=True), jnp.max(s2, axis=1, keepdims=True)
        )
        p1, p2 = jnp.exp(s1 - top), jnp.exp(s2 - top)
        total = jnp.sum(p1, axis=1, keepdims=True) + jnp.sum(p2, axis=1, keepdims=True)
        o = jnp.dot(p1.astype(BF16), vbuf[:, :, h].reshape(1024, 256), preferred_element_type=F32)
        o = o + jnp.dot(p2.astype(BF16), vs[h], preferred_element_type=F32)
        o = o * in_group4
        o = o[:, :128] + o[:, 128:]
        o = (o + pltpu.roll(o, 64, 1)) * (1.0 / total)
        left, right = jnp.where(low, o[0:128], o[128:256]), jnp.where(low, o[256:384], o[384:512])
        attn[:, lanes] = jnp.concatenate([left, right], axis=1).astype(BF16)
        return carry

    lax.fori_loop(0, 4, head, 0)

    up2.relay()
    down1.finish()
    local_down.wait()
    down2.start()
    down_share = [send(wd.at[x, c], wd.at[x, c], partner)]
    for i in up2.around()[:2]:
        up_share.append(send(wu.at[:, i, c], wu.at[:, i, c], partner))

    local_out.wait()
    local_res.wait()

    def project(n, square):
        lanes = pl.ds(pl.multiple_of(n * 256, 256), 256)
        part = resb[:, lanes].astype(F32) + jnp.dot(
            attn[...], owb[:, lanes], preferred_element_type=F32
        )
        hid[:, lanes] = part
        return square + jnp.sum(part * part, axis=1, keepdims=True)

    square = lax.fori_loop(0, 8, project, jnp.zeros((128, 1), F32))
    scale = lax.rsqrt(square * (1.0 / 2048) + EPSILON)
    xn[0] = (hid[...] * scale * gain_in[...]).astype(BF16)

    tok_up = send(xn.at[0], xn.at[3], zs[1])
    tok_down = send(xn.at[0], xn.at[1], zs[-1])
    tok_up.wait_recv()
    tok_a = send(xn.at[3, pl.ds(0, 64)], xn.at[2, pl.ds(0, 64)], zs[1])
    tok_down.wait_recv()
    tok_b = send(xn.at[1, pl.ds(64, 64)], xn.at[2, pl.ds(64, 64)], zs[-1])

    gate2.relay()
    for i in gate2.around()[:2]:
        gate_share.append(send(wg.at[i, :, c], wg.at[i, :, c], partner))
    up2.finish()
    i = up2.around()[2]
    up_share.append(send(wu.at[:, i, c], wu.at[:, i, c], partner))
    down2.relay()
    for i in down2.around()[:2]:
        down_share.append(send(wd.at[i, c], wd.at[i, c], partner))
    gate2.finish()
    i = gate2.around()[2]
    gate_share.append(send(wg.at[i, :, c], wg.at[i, :, c], partner))
    tok_a.wait_recv()
    tok_b.wait_recv()
    for copy in up_share + gate_share:
        copy.wait_recv()

    def hidden_units(i, carry):
        block, cols = i // 2, pl.ds(pl.multiple_of(lax.rem(i, 2) * 256, 256), 256)
        tokens = xn[...].reshape(512, 2048)
        g = jnp.dot(tokens, wg[block, :, :, :, cols].reshape(2048, 256), preferred_element_type=F32)
        u = jnp.dot(tokens, wu[block, :, :, :, cols].reshape(2048, 256), preferred_element_type=F32)
        act[:, pl.ds(pl.multiple_of(i * 256, 256), 256)] = (g / (1.0 + jnp.exp(-g)) * u).astype(BF16)
        return carry

    lax.fori_loop(0, 8, hidden_units, 0)

    returns = []

    def down_columns(i):
        for cc in range(2):
            block = i * 2 + cc
            part = jnp.dot(act[...], wd[i, cc].reshape(2048, 256), preferred_element_type=F32)
            acc[block] = part[0:128]
            for k in (1, 2, 3):
                stage[k, block] = part[128 * k:128 * k + 128].astype(BF16)
                target = zs[{1: 1, 2: 2, 3: -1}[k]]
                returns.append(send(stage.at[k, block], back.at[4 - k, block], target))

    down_share[0].wait_recv()
    down_columns(x)
    a, b, far = down2.around()
    down_share[1].wait_recv()
    down_columns(a)
    down_share[2].wait_recv()
    down_columns(b)
    down2.finish()
    down_share.append(send(wd.at[far, c], wd.at[far, c], partner))
    down_share[3].wait_recv()
    down_columns(far)

    for copy in returns:
        copy.wait_recv()
    for n in range(8):
        lanes = slice(256 * n, 256 * n + 256)
        terms = acc[n] + back[1, n].astype(F32) + back[2, n].astype(F32) + back[3, n].astype(F32)
        out[:, lanes] = (hid[:, lanes] + terms).astype(BF16)

    for copy in started:
        copy.wait_send()


def shards(
    residual, queries, keys, values, prefix_keys, cached_prefix_values, out_weight, norm_gain,
    w_gate, w_up, w_down, suffix_lengths, request_group, placement_order,
):
    vmem = pl.BlockSpec(memory_space=pltpu.VMEM)
    anywhere = pl.BlockSpec(memory_space=pl.ANY)
    return pl.pallas_call(
        kernel,
        out_shape=jax.ShapeDtypeStruct((128, 2048), BF16),
        in_specs=[
            anywhere, vmem, vmem, vmem, vmem, vmem, anywhere, vmem,
            anywhere, anywhere, anywhere, vmem, vmem, vmem,
        ],
        out_specs=vmem,
        scratch_shapes=[
            pltpu.VMEM((4, 4, 4, 64, 256), BF16),
            pltpu.VMEM((4, 4, 4, 64, 256), BF16),
            pltpu.VMEM((128, 256), BF16),
            pltpu.VMEM((128, 256), BF16),
            pltpu.VMEM((4, 256, 256), BF16),
            pltpu.VMEM((4, 256, 256), BF16),
            pltpu.VMEM((128, 1024), BF16),
            pltpu.VMEM((1024, 2048), BF16),
            pltpu.VMEM((128, 2048), BF16),
            pltpu.VMEM((128, 2048), F32),
            pltpu.VMEM((4, 128, 2048), BF16),
            pltpu.VMEM((4, 4, 2, 256, 512), BF16),
            pltpu.VMEM((4, 4, 2, 256, 512), BF16),
            pltpu.VMEM((4, 2, 4, 512, 256), BF16),
            pltpu.VMEM((512, 2048), BF16),
            pltpu.VMEM((8, 128, 256), F32),
            pltpu.VMEM((4, 8, 128, 256), BF16),
            pltpu.VMEM((4, 8, 128, 256), BF16),
            pltpu.SemaphoreType.DMA((N_SEM,)),
            pltpu.SemaphoreType.DMA((N_SEM,)),
            pltpu.SemaphoreType.DMA((5,)),
        ],
        compiler_params=pltpu.CompilerParams(
            collective_id=0, has_side_effects=True, vmem_limit_bytes=63 << 20
        ),
    )(
        residual, queries, keys, values, prefix_keys, cached_prefix_values, out_weight,
        norm_gain.reshape(1, -1), w_gate, w_up, w_down,
        suffix_lengths, request_group, placement_order,
    )


def solution(mesh):
    placed = (
        P(("grp", "dev"), None),
        P(("grp", "dev"), None),
        P(("grp", "dev"), None),
        P(("grp", "dev"), None),
        P("grp", "dev", None),
        P("grp", "dev", None),
        P(),
        P(),
        P("grp", "dev"),
        P("grp", "dev"),
        P("dev", "grp"),
        P("grp", None),
        P("grp", None),
        P("grp", None),
    )
    return jax.shard_map(
        shards, mesh=mesh, in_specs=placed, out_specs=P(("grp", "dev"), None), check_vma=False
    )
```

```python
import jax
import jax.numpy as jnp
from jax import lax
from jax.experimental import pallas as pl
from jax.experimental.pallas import tpu as pltpu
from jax.sharding import PartitionSpec as P

EPSILON = 1e-05
NEG_FILL = -1e30
MESH = pl.DeviceIdType.MESH
F32, BF16 = jnp.float32, jnp.bfloat16
N_SEM = 136


def token_info(lengths, groups, order, first_row):
    n = lengths.shape[1]
    rows = lax.broadcasted_iota(jnp.int32, (n, n), 0)
    cols = lax.broadcasted_iota(jnp.int32, (n, n), 1)
    diagonal = rows == cols

    def column(row):
        spread = jnp.broadcast_to(row, (n, n))
        return jnp.sum(jnp.where(diagonal, spread, 0.0), axis=1, keepdims=True)

    picked = jnp.broadcast_to(order, (n, n)) == rows
    packed_len = jnp.sum(jnp.where(picked, column(lengths), 0.0), axis=0, keepdims=True)
    packed_group = jnp.sum(jnp.where(picked, column(groups), 0.0), axis=0, keepdims=True)
    ends = jnp.sum(jnp.where(rows <= cols, column(packed_len), 0.0), axis=0, keepdims=True)
    starts = ends - packed_len
    token = (lax.broadcasted_iota(jnp.int32, (128, n), 0) + first_row).astype(F32)
    inside = (token >= starts) & (token < ends)
    group = jnp.sum(jnp.where(inside, packed_group, 0.0), axis=1, keepdims=True)
    start = jnp.sum(jnp.where(inside, starts, 0.0), axis=1, keepdims=True)
    return group, start


def kernel(
    res_in, q_in, k_in, v_in, pk_in, pv_in, ow_in, gain_in, wg_in, wu_in, wd_in, len_in, grp_in, ord_in,
    out,
    kbuf, vbuf, zk, zv, sk, sv, kprev, vprev, ks, vs, attn, owb, res, hid, xn, wg, wu, wda, wdb, upv, act,
    acc, ends, far, hop, near, back,
    ssem, rsem, lsem,
):
    gi, di = lax.axis_index("grp"), lax.axis_index("dev")
    x, c = gi // 2, lax.rem(gi, 2)
    z, y = di // 4, lax.rem(di, 4)

    def at(xx, cc, zz, yy):
        return (lax.rem(xx + 4, 4) * 2 + cc, lax.rem(zz + 4, 4) * 4 + lax.rem(yy + 4, 4))

    xs = {k: at(x + k, c, z, y) for k in (1, -1)}
    ys = {k: at(x, c, z, y + k) for k in (1, -1)}
    zs = {k: at(x, c, z + k, y) for k in (1, -1)}
    partner = (x * 2 + (1 - c), di)
    peers = [xs[1], xs[-1], ys[1], ys[-1], zs[1], zs[-1], partner]

    barrier = pltpu.get_barrier_semaphore()
    for peer in peers:
        pl.semaphore_signal(barrier, inc=1, device_id=peer, device_id_type=MESH)

    started = []
    counter = [0]

    def send(src, dst, device):
        i = counter[0]
        counter[0] += 1
        copy = pltpu.make_async_remote_copy(
            src_ref=src, dst_ref=dst, send_sem=ssem.at[i], recv_sem=rsem.at[i],
            device_id=device, device_id_type=MESH,
        )
        copy.start()
        started.append(copy)
        return copy

    local_count = [0]

    def bring(src, dst):
        i = local_count[0]
        local_count[0] += 1
        copy = pltpu.make_async_copy(src, dst, lsem.at[i])
        copy.start()
        return copy

    class Ring:
        def __init__(self, where, pos, slot, half):
            self.where, self.pos, self.slot, self.half = where, pos, slot, half

        def start(self, src=None):
            mine = self.slot(self.pos)
            src = mine if src is None else src
            self.up = send(src, mine, self.where[1])
            self.down = send(src, mine, self.where[-1])

        def relay(self):
            before, after = lax.rem(self.pos + 3, 4), lax.rem(self.pos + 1, 4)
            self.up.wait_recv()
            self.a = send(self.half(before, 0), self.half(before, 0), self.where[1])
            self.down.wait_recv()
            self.b = send(self.half(after, 1), self.half(after, 1), self.where[-1])

        def finish(self):
            self.a.wait_recv()
            self.b.wait_recv()

        def around(self):
            return [lax.rem(self.pos + k, 4) for k in (3, 1, 2)]

    class Piece:
        def __init__(self, first, second, src, local):
            self.first, self.second, self.src, self.local = first, second, src, local
            self.shared = []

        def share(self, i):
            block = self.second.slot(i)
            self.shared.append(send(block, block, partner))

        def start(self):
            self.first.start(self.src)

        def relay1(self):
            self.first.relay()

        def finish1(self):
            self.first.finish()
            if self.local is not None:
                self.local.wait()
            self.share(self.second.pos)

        def turn(self):
            self.second.start()

        def relay2(self):
            self.second.relay()
            for i in self.second.around()[:2]:
                self.share(i)

        def finish2(self):
            self.second.finish()
            self.share(self.second.around()[2])

        def ready(self, n=None):
            for copy in self.shared[:n] if n is not None else self.shared:
                copy.wait_recv()
            self.shared = self.shared[n:] if n is not None else []

    local_gate = bring(wg_in, wg.at[y, x, c])
    local_up = bring(wu_in, wu.at[y, x, c])
    local_da = bring(wd_in.at[:, pl.ds(0, 128)], wda.at[c, x, y])
    local_db = bring(wd_in.at[:, pl.ds(128, 128)], wdb.at[c, x, y])
    local_res = bring(res_in, res.at[0])
    local_out = bring(ow_in, owb)

    top, bottom = pl.ds(0, 128), pl.ds(128, 128)

    def quarter(lo, h):
        return pl.ds(lo + 64 * h, 64)

    gate_a = Piece(
        Ring(xs, x, lambda i: wg.at[y, i, c, top], lambda i, h: wg.at[y, i, c, quarter(0, h)]),
        Ring(ys, y, lambda i: wg.at[i, :, c, top], lambda i, h: wg.at[i, pl.ds(2 * h, 2), c, top]),
        wg_in.at[top], local_gate,
    )
    gate_b = Piece(
        Ring(ys, y, lambda i: wg.at[i, x, c, bottom], lambda i, h: wg.at[i, x, c, quarter(128, h)]),
        Ring(xs, x, lambda i: wg.at[:, i, c, bottom], lambda i, h: wg.at[pl.ds(2 * h, 2), i, c, bottom]),
        wg_in.at[bottom], None,
    )
    up_a = Piece(
        Ring(ys, y, lambda i: wu.at[i, x, c, top], lambda i, h: wu.at[i, x, c, quarter(0, h)]),
        Ring(xs, x, lambda i: wu.at[:, i, c, top], lambda i, h: wu.at[pl.ds(2 * h, 2), i, c, top]),
        wu_in.at[top], local_up,
    )
    up_b = Piece(
        Ring(ys, y, lambda i: wu.at[i, x, c, bottom], lambda i, h: wu.at[i, x, c, quarter(128, h)]),
        Ring(xs, x, lambda i: wu.at[:, i, c, bottom], lambda i, h: wu.at[pl.ds(2 * h, 2), i, c, bottom]),
        wu_in.at[bottom], None,
    )
    down_a = Piece(
        Ring(xs, x, lambda i: wda.at[c, i, y], lambda i, h: wda.at[c, i, y, pl.ds(256 * h, 256)]),
        Ring(ys, y, lambda i: wda.at[c, :, i], lambda i, h: wda.at[c, pl.ds(2 * h, 2), i]),
        wd_in.at[:, pl.ds(0, 128)], local_da,
    )
    down_b = Piece(
        Ring(ys, y, lambda i: wdb.at[c, x, i], lambda i, h: wdb.at[c, x, i, pl.ds(256 * h, 256)]),
        Ring(xs, x, lambda i: wdb.at[c, i], lambda i, h: wdb.at[c, i, pl.ds(2 * h, 2)]),
        wd_in.at[:, pl.ds(128, 128)], local_db,
    )
    key1 = Ring(ys, y, lambda i: kbuf.at[z, i], lambda i, h: kbuf.at[z, i, pl.ds(2 * h, 2)])
    key2 = Ring(zs, z, lambda i: kbuf.at[i], lambda i, h: kbuf.at[i, pl.ds(2 * h, 2)])
    val1 = Ring(zs, z, lambda i: vbuf.at[i, y], lambda i, h: vbuf.at[i, y, pl.ds(2 * h, 2)])
    val2 = Ring(ys, y, lambda i: vbuf.at[:, i], lambda i, h: vbuf.at[pl.ds(2 * h, 2), i])

    low64 = lax.broadcasted_iota(jnp.int32, (64, 128), 1) < 64
    for src, dst in ((pk_in, kbuf), (pv_in, vbuf)):
        for h in range(4):
            cut = slice(128 * (h // 2), 128 * (h // 2) + 128)
            pairs = []
            for g in (0, 2):
                a, b = src[g, :, cut].astype(F32), src[g + 1, :, cut].astype(F32)
                if h % 2 == 0:
                    pairs.append(jnp.where(low64, a, pltpu.roll(b, 64, 1)))
                else:
                    pairs.append(jnp.where(low64, pltpu.roll(a, 64, 1), b))
            dst[z, y, h] = jnp.concatenate(pairs, axis=1).astype(BF16)

    pl.semaphore_wait(barrier, len(peers))
    key1.start()
    val1.start()
    gate_a.start()
    up_a.start()
    up_b.start()
    down_a.start()
    over_k = send(k_in, zk, zs[1])
    over_v = send(v_in, zv, zs[1])

    first_row = di * 128
    group, start = token_info(
        len_in[...].astype(F32), grp_in[...].astype(F32), ord_in[...], first_row
    )
    lane_group = (lax.broadcasted_iota(jnp.int32, (128, 256), 1) // 64).astype(F32)
    in_group = (lane_group == group).astype(F32)
    window = (lax.broadcasted_iota(jnp.int32, (128, 256), 1) + (first_row - 128)).astype(F32)
    token = (lax.broadcasted_iota(jnp.int32, (128, 256), 0) + first_row).astype(F32)
    bias = jnp.where((window >= start) & (window <= token), 0.0, NEG_FILL)
    low = lax.broadcasted_iota(jnp.int32, (128, 128), 1) < 64

    def twice(block):
        turned = pltpu.roll(block, 64, 1)
        first, second = jnp.where(low, block, turned), jnp.where(low, turned, block)
        return jnp.concatenate([first, first], axis=1), jnp.concatenate([second, second], axis=1)

    def spread(src, dst, row):
        for b in (0, 1):
            first, second = twice(src[:, 128 * b:128 * b + 128].astype(F32))
            dst[2 * b, row:row + 128] = first.astype(BF16)
            dst[2 * b + 1, row:row + 128] = second.astype(BF16)

    key1.relay()
    val1.relay()
    up_a.relay1()
    up_b.relay1()
    gate_a.relay1()
    val1.finish()
    val2.start()
    key1.finish()
    key2.start()
    gate_b.start()
    up_a.finish1()
    up_a.turn()
    up_b.finish1()
    up_b.turn()
    down_a.relay1()

    over_k.wait_recv()
    over_v.wait_recv()
    edge = (y == 3).astype(F32)
    for src, over, staged in ((k_in, zk, sk), (v_in, zv, sv)):
        staged[...] = (
            over[...].astype(F32) * edge + src[...].astype(F32) * (1.0 - edge)
        ).astype(BF16)
    next_k = send(sk, kprev, ys[1])
    next_v = send(sv, vprev, ys[1])
    spread(k_in, ks, 128)
    spread(v_in, vs, 128)

    gate_a.finish1()
    down_a.finish1()
    key2.relay()
    val2.relay()
    down_b.start()
    gate_b.relay1()
    local_res.wait()
    tokens_up = send(res.at[0], res.at[3], zs[1])
    tokens_down = send(res.at[0], res.at[1], zs[-1])
    next_k.wait_recv()
    next_v.wait_recv()
    spread(kprev, ks, 0)
    spread(vprev, vs, 0)
    up_a.relay2()
    gate_a.turn()
    key2.finish()
    val2.finish()

    bias4 = jnp.concatenate([bias] * 4, axis=0)
    in_group4 = jnp.concatenate([in_group] * 4, axis=0)

    def head(h):
        lanes = slice(256 * h, 256 * h + 256)
        block = q_in[:, lanes].astype(F32) * 0.125
        rows = [part * in_group for b in (0, 1) for part in twice(block[:, 128 * b:128 * b + 128])]
        qx = jnp.concatenate(rows, axis=0).astype(BF16)
        keys = kbuf[:, :, h].reshape(1024, 256)
        contract = (((1,), (1,)), ((), ()))
        s1 = lax.dot_general(qx, keys, contract, preferred_element_type=F32)
        s2 = lax.dot_general(qx, ks[h], contract, preferred_element_type=F32) + bias4
        peak = jnp.maximum(
            jnp.max(s1, axis=1, keepdims=True), jnp.max(s2, axis=1, keepdims=True)
        )
        p1, p2 = jnp.exp(s1 - peak), jnp.exp(s2 - peak)
        total = jnp.sum(p1, axis=1, keepdims=True) + jnp.sum(p2, axis=1, keepdims=True)
        o = jnp.dot(p1.astype(BF16), vbuf[:, :, h].reshape(1024, 256), preferred_element_type=F32)
        o = o + jnp.dot(p2.astype(BF16), vs[h], preferred_element_type=F32)
        o = o * in_group4
        o = o[:, :128] + o[:, 128:]
        o = (o + pltpu.roll(o, 64, 1)) * (1.0 / total)
        left, right = jnp.where(low, o[0:128], o[128:256]), jnp.where(low, o[256:384], o[384:512])
        attn[0, :, lanes] = jnp.concatenate([left, right], axis=1).astype(BF16)

    def pair_start(p):
        lanes = pl.ds(512 * p, 512)
        return [
            send(attn.at[0, :, lanes], attn.at[3, :, lanes], zs[1]),
            send(attn.at[0, :, lanes], attn.at[1, :, lanes], zs[-1]),
        ]

    def onward(buf, copies, lanes):
        copies[0].wait_recv()
        a = send(buf.at[3, pl.ds(0, 64), lanes], buf.at[2, pl.ds(0, 64), lanes], zs[1])
        copies[1].wait_recv()
        b = send(buf.at[1, pl.ds(64, 64), lanes], buf.at[2, pl.ds(64, 64), lanes], zs[-1])
        return [a, b]

    head(0)
    head(1)
    pair0 = pair_start(0)
    up_b.relay2()
    gate_b.finish1()
    gate_b.turn()
    head(2)
    res_far = onward(res, [tokens_up, tokens_down], pl.ds(0, 2048))
    head(3)
    pair1 = pair_start(1)
    pair0 = onward(attn, pair0, pl.ds(0, 512))
    down_b.relay1()
    up_a.finish2()
    pair1 = onward(attn, pair1, pl.ds(512, 512))
    up_b.finish2()
    for copy in res_far + pair0 + pair1:
        copy.wait_recv()
    local_out.wait()

    def project(n, square):
        lanes = pl.ds(pl.multiple_of(n * 256, 256), 256)
        part = res[:, :, lanes].reshape(512, 256).astype(F32) + jnp.dot(
            attn[...].reshape(512, 1024), owb[:, lanes], preferred_element_type=F32
        )
        hid[:, lanes] = part
        return square + jnp.sum(part * part, axis=1, keepdims=True)

    square = lax.fori_loop(0, 8, project, jnp.zeros((512, 1), F32))
    scale = lax.rsqrt(square * (1.0 / 2048) + EPSILON)

    def normalize(n, carry):
        lanes = pl.ds(pl.multiple_of(n * 256, 256), 256)
        xn[:, lanes] = (hid[:, lanes] * scale * gain_in[:, lanes]).astype(BF16)
        return carry

    lax.fori_loop(0, 8, normalize, 0)

    up_a.ready()
    up_b.ready()

    def up_units(i, carry):
        block, cols = i // 2, pl.ds(pl.multiple_of(lax.rem(i, 2) * 256, 256), 256)
        upv[i] = jnp.dot(
            xn[...], wu[block, :, :, :, cols].reshape(2048, 256), preferred_element_type=F32
        )
        return carry

    lax.fori_loop(0, 4, up_units, 0)
    gate_a.relay2()
    down_a.turn()
    down_b.finish1()
    lax.fori_loop(4, 8, up_units, 0)
    gate_b.relay2()
    down_b.turn()
    gate_a.finish2()
    gate_b.finish2()
    gate_a.ready()
    gate_b.ready()

    def gate_units(i, carry):
        block, cols = i // 2, pl.ds(pl.multiple_of(lax.rem(i, 2) * 256, 256), 256)
        g = jnp.dot(
            xn[...], wg[block, :, :, :, cols].reshape(2048, 256), preferred_element_type=F32
        )
        act[:, pl.ds(pl.multiple_of(i * 256, 256), 256)] = (
            g / (1.0 + jnp.exp(-g)) * upv[i]
        ).astype(BF16)
        return carry

    lax.fori_loop(0, 8, gate_units, 0)

    half0, half1 = pl.ds(0, 64), pl.ds(64, 64)
    hops, returns = {}, []

    def block_sums(half, i):
        weight = (wda, wdb)[half]
        part = jnp.dot(
            act[...],
            jnp.concatenate([weight[0, i].reshape(2048, 128), weight[1, i].reshape(2048, 128)], axis=1),
            preferred_element_type=F32,
        )
        n = half * 4 + i
        acc[n] = part[0:128]
        ends[0, n] = part[128:256]
        ends[1, n] = part[384:512]
        far[n] = part[256:384].astype(BF16)
        hops[len(hops)] = (
            n,
            send(far.at[n, half0], hop.at[0, n], zs[1]),
            send(far.at[n, half1], hop.at[1, n], zs[-1]),
        )

    def pass_on(k):
        n, a, b = hops[k]
        a.wait_recv()
        near[0, n, 0:64] = (ends[0, n, 0:64] + hop[0, n].astype(F32)).astype(BF16)
        near[0, n, 64:128] = ends[0, n, 64:128].astype(BF16)
        returns.append(send(near.at[0, n], back.at[0, n], zs[1]))
        b.wait_recv()
        near[1, n, 0:64] = ends[1, n, 0:64].astype(BF16)
        near[1, n, 64:128] = (ends[1, n, 64:128] + hop[1, n].astype(F32)).astype(BF16)
        returns.append(send(near.at[1, n], back.at[1, n], zs[-1]))

    before, after, opposite = [lax.rem(x + k, 4) for k in (3, 1, 2)]
    down_b.ready(1)
    block_sums(1, x)
    down_b.relay2()
    down_a.relay2()
    down_b.ready(2)
    block_sums(1, before)
    pass_on(0)
    block_sums(1, after)
    pass_on(1)
    down_a.finish2()
    down_a.ready()
    for step, i in enumerate((x, before, after, opposite)):
        block_sums(0, i)
        pass_on(2 + step)
    down_b.finish2()
    down_b.ready()
    block_sums(1, opposite)
    pass_on(6)
    pass_on(7)

    for copy in returns:
        copy.wait_recv()
    for half in range(2):
        for i in range(4):
            n = half * 4 + i
            total = acc[n] + back[0, n].astype(F32) + back[1, n].astype(F32)
            for cc in range(2):
                lanes = slice(512 * i + 256 * cc + 128 * half, 512 * i + 256 * cc + 128 * half + 128)
                out[:, lanes] = (hid[0:128, lanes] + total[:, 128 * cc:128 * cc + 128]).astype(BF16)

    for copy in started:
        copy.wait_send()
    assert counter[0] == N_SEM, counter[0]


def shards(
    residual, queries, keys, values, prefix_keys, cached_prefix_values, out_weight, norm_gain,
    w_gate, w_up, w_down, suffix_lengths, request_group, placement_order,
):
    vmem = pl.BlockSpec(memory_space=pltpu.VMEM)
    anywhere = pl.BlockSpec(memory_space=pl.ANY)
    return pl.pallas_call(
        kernel,
        out_shape=jax.ShapeDtypeStruct((128, 2048), BF16),
        in_specs=[
            anywhere, vmem, vmem, vmem, vmem, vmem, anywhere, vmem,
            anywhere, anywhere, anywhere, vmem, vmem, vmem,
        ],
        out_specs=vmem,
        scratch_shapes=[
            pltpu.VMEM((4, 4, 4, 64, 256), BF16),
            pltpu.VMEM((4, 4, 4, 64, 256), BF16),
            pltpu.VMEM((128, 256), BF16),
            pltpu.VMEM((128, 256), BF16),
            pltpu.VMEM((128, 256), BF16),
            pltpu.VMEM((128, 256), BF16),
            pltpu.VMEM((128, 256), BF16),
            pltpu.VMEM((128, 256), BF16),
            pltpu.VMEM((4, 256, 256), BF16),
            pltpu.VMEM((4, 256, 256), BF16),
            pltpu.VMEM((4, 128, 1024), BF16),
            pltpu.VMEM((1024, 2048), BF16),
            pltpu.VMEM((4, 128, 2048), BF16),
            pltpu.VMEM((512, 2048), F32),
            pltpu.VMEM((512, 2048), BF16),
            pltpu.VMEM((4, 4, 2, 256, 512), BF16),
            pltpu.VMEM((4, 4, 2, 256, 512), BF16),
            pltpu.VMEM((2, 4, 4, 512, 128), BF16),
            pltpu.VMEM((2, 4, 4, 512, 128), BF16),
            pltpu.VMEM((8, 512, 256), F32),
            pltpu.VMEM((512, 2048), BF16),
            pltpu.VMEM((8, 128, 256), F32),
            pltpu.VMEM((2, 8, 128, 256), F32),
            pltpu.VMEM((8, 128, 256), BF16),
            pltpu.VMEM((2, 8, 64, 256), BF16),
            pltpu.VMEM((2, 8, 128, 256), BF16),
            pltpu.VMEM((2, 8, 128, 256), BF16),
            pltpu.SemaphoreType.DMA((N_SEM,)),
            pltpu.SemaphoreType.DMA((N_SEM,)),
            pltpu.SemaphoreType.DMA((6,)),
        ],
        compiler_params=pltpu.CompilerParams(
            collective_id=0, has_side_effects=True, vmem_limit_bytes=63 << 20
        ),
    )(
        residual, queries, keys, values, prefix_keys, cached_prefix_values, out_weight,
        norm_gain.reshape(1, -1), w_gate, w_up, w_down,
        suffix_lengths, request_group, placement_order,
    )


def solution(mesh):
    placed = (
        P(("grp", "dev"), None),
        P(("grp", "dev"), None),
        P(("grp", "dev"), None),
        P(("grp", "dev"), None),
        P("grp", "dev", None),
        P("grp", "dev", None),
        P(),
        P(),
        P("grp", "dev"),
        P("grp", "dev"),
        P("dev", "grp"),
        P("grp", None),
        P("grp", None),
        P("grp", None),
    )
    return jax.shard_map(
        shards, mesh=mesh, in_specs=placed, out_specs=P(("grp", "dev"), None), check_vma=False
    )
```

```python
import jax
import jax.numpy as jnp
from jax import lax
from jax.experimental import pallas as pl
from jax.experimental.pallas import tpu as pltpu
from jax.sharding import PartitionSpec as P

EPSILON = 1e-05
NEG_FILL = -1e30
MESH = pl.DeviceIdType.MESH
F32, BF16 = jnp.float32, jnp.bfloat16
N_SEM = 164


def token_info(lengths, groups, order, first_row):
    n = lengths.shape[1]
    rows = lax.broadcasted_iota(jnp.int32, (n, n), 0)
    cols = lax.broadcasted_iota(jnp.int32, (n, n), 1)
    diagonal = rows == cols

    def column(row):
        spread = jnp.broadcast_to(row, (n, n))
        return jnp.sum(jnp.where(diagonal, spread, 0.0), axis=1, keepdims=True)

    picked = jnp.broadcast_to(order, (n, n)) == rows
    packed_len = jnp.sum(jnp.where(picked, column(lengths), 0.0), axis=0, keepdims=True)
    packed_group = jnp.sum(jnp.where(picked, column(groups), 0.0), axis=0, keepdims=True)
    ends = jnp.sum(jnp.where(rows <= cols, column(packed_len), 0.0), axis=0, keepdims=True)
    starts = ends - packed_len
    token = (lax.broadcasted_iota(jnp.int32, (128, n), 0) + first_row).astype(F32)
    inside = (token >= starts) & (token < ends)
    group = jnp.sum(jnp.where(inside, packed_group, 0.0), axis=1, keepdims=True)
    start = jnp.sum(jnp.where(inside, starts, 0.0), axis=1, keepdims=True)
    return group, start


def kernel(
    res_in, q_in, k_in, v_in, pk_in, pv_in, ow_in, gain_in, wg_in, wu_in, wd_in, len_in, grp_in, ord_in,
    out,
    kbuf, vbuf, zk, zv, sk, sv, kprev, vprev, ks, vs, attn, owb, res, hid, xn, wg, wu, wd, upv, act,
    acc, ends, far, hop, near, back,
    ssem, rsem, lsem,
):
    gi, di = lax.axis_index("grp"), lax.axis_index("dev")
    x, c = gi // 2, lax.rem(gi, 2)
    z, y = di // 4, lax.rem(di, 4)

    def at(xx, cc, zz, yy):
        return (lax.rem(xx + 4, 4) * 2 + cc, lax.rem(zz + 4, 4) * 4 + lax.rem(yy + 4, 4))

    xs = {k: at(x + k, c, z, y) for k in (1, -1)}
    ys = {k: at(x, c, z, y + k) for k in (1, -1)}
    zs = {k: at(x, c, z + k, y) for k in (1, -1)}
    partner = (x * 2 + (1 - c), di)
    peers = [xs[1], xs[-1], ys[1], ys[-1], zs[1], zs[-1], partner]

    barrier = pltpu.get_barrier_semaphore()
    for peer in peers:
        pl.semaphore_signal(barrier, inc=1, device_id=peer, device_id_type=MESH)

    started = []
    counter = [0]

    class Copy:
        def __init__(self, src, dst, device, i):
            self.src, self.dst, self.device, self.i = src, dst, device, i

        def copy(self):
            src, dst = [ref() if callable(ref) else ref for ref in (self.src, self.dst)]
            return pltpu.make_async_remote_copy(
                src_ref=src, dst_ref=dst, send_sem=ssem.at[self.i], recv_sem=rsem.at[self.i],
                device_id=self.device, device_id_type=MESH,
            )

        def start(self):
            self.copy().start()

        def wait_recv(self):
            self.copy().wait_recv()

        def wait_send(self):
            self.copy().wait_send()

    def send(src, dst, device):
        copy = Copy(src, dst, device, counter[0])
        counter[0] += 1
        copy.start()
        started.append(copy)
        return copy

    local_count = [0]

    def bring(src, dst):
        i = local_count[0]
        local_count[0] += 1
        copy = pltpu.make_async_copy(src, dst, lsem.at[i])
        copy.start()
        return copy

    class Ring:
        def __init__(self, where, pos, slot, half):
            self.where, self.pos, self.slot, self.half = where, pos, slot, half
            self.before, self.after, self.far = [lax.rem(pos + k, 4) for k in (3, 1, 2)]

        def start(self, src=None):
            mine = lambda: self.slot(self.pos)
            src = mine if src is None else src
            self.up = send(src, mine, self.where[1])
            self.down = send(src, mine, self.where[-1])

        def relay(self):
            before, after = self.before, self.after
            self.up.wait_recv()
            first, second = lambda: self.half(before, 0), lambda: self.half(after, 1)
            self.a = send(first, first, self.where[1])
            self.down.wait_recv()
            self.b = send(second, second, self.where[-1])

        def finish(self):
            self.a.wait_recv()
            self.b.wait_recv()

        def around(self):
            return [self.before, self.after, self.far]

    class Piece:
        def __init__(self, first, second, src, local):
            self.first, self.second, self.src, self.local = first, second, src, local
            self.shared = []

        def share(self, i):
            block = lambda: self.second.slot(i)
            self.shared.append(send(block, block, partner))

        def start(self):
            self.first.start(self.src)

        def relay1(self):
            self.first.relay()

        def finish1(self):
            self.first.finish()
            if self.local is not None:
                self.local.wait()
            self.share(self.second.pos)

        def turn(self):
            self.second.start()

        def relay2(self):
            self.second.relay()
            for i in self.second.around()[:2]:
                self.share(i)

        def finish2(self):
            self.second.finish()
            self.share(self.second.around()[2])

        def ready(self, n=None):
            for copy in self.shared[:n] if n is not None else self.shared:
                copy.wait_recv()
            self.shared = self.shared[n:] if n is not None else []

    local_gate = bring(wg_in, wg.at[y, x, c])
    local_up = bring(wu_in, wu.at[y, x, c])
    local_da = bring(wd_in.at[:, pl.ds(0, 128)], wd.at[0, c, x, y])
    local_db = bring(wd_in.at[:, pl.ds(128, 128)], wd.at[1, c, x, y])
    local_res = bring(res_in, res.at[0])
    local_out = bring(ow_in, owb)

    top, bottom = pl.ds(0, 128), pl.ds(128, 128)

    def quarter(lo, h):
        return pl.ds(lo + 64 * h, 64)

    gate_a = Piece(
        Ring(xs, x, lambda i: wg.at[y, i, c, top], lambda i, h: wg.at[y, i, c, quarter(0, h)]),
        Ring(ys, y, lambda i: wg.at[i, :, c, top], lambda i, h: wg.at[i, pl.ds(2 * h, 2), c, top]),
        wg_in.at[top], local_gate,
    )
    gate_b = Piece(
        Ring(ys, y, lambda i: wg.at[i, x, c, bottom], lambda i, h: wg.at[i, x, c, quarter(128, h)]),
        Ring(xs, x, lambda i: wg.at[:, i, c, bottom], lambda i, h: wg.at[pl.ds(2 * h, 2), i, c, bottom]),
        wg_in.at[bottom], None,
    )
    up_a = Piece(
        Ring(ys, y, lambda i: wu.at[i, x, c, top], lambda i, h: wu.at[i, x, c, quarter(0, h)]),
        Ring(xs, x, lambda i: wu.at[:, i, c, top], lambda i, h: wu.at[pl.ds(2 * h, 2), i, c, top]),
        wu_in.at[top], local_up,
    )
    up_b = Piece(
        Ring(ys, y, lambda i: wu.at[i, x, c, bottom], lambda i, h: wu.at[i, x, c, quarter(128, h)]),
        Ring(xs, x, lambda i: wu.at[:, i, c, bottom], lambda i, h: wu.at[pl.ds(2 * h, 2), i, c, bottom]),
        wu_in.at[bottom], None,
    )
    down_a = Piece(
        Ring(xs, x, lambda i: wd.at[0, c, i, y], lambda i, h: wd.at[0, c, i, y, pl.ds(256 * h, 256)]),
        Ring(ys, y, lambda i: wd.at[0, c, :, i], lambda i, h: wd.at[0, c, pl.ds(2 * h, 2), i]),
        wd_in.at[:, pl.ds(0, 128)], local_da,
    )
    down_b = Piece(
        Ring(ys, y, lambda i: wd.at[1, c, x, i], lambda i, h: wd.at[1, c, x, i, pl.ds(256 * h, 256)]),
        Ring(xs, x, lambda i: wd.at[1, c, i], lambda i, h: wd.at[1, c, i, pl.ds(2 * h, 2)]),
        wd_in.at[:, pl.ds(128, 128)], local_db,
    )
    key1 = Ring(ys, y, lambda i: kbuf.at[z, i], lambda i, h: kbuf.at[z, i, pl.ds(2 * h, 2)])
    val1 = Ring(zs, z, lambda i: vbuf.at[i, y], lambda i, h: vbuf.at[i, y, pl.ds(2 * h, 2)])

    def pair_rings(heads):
        key = Ring(
            zs, z, lambda i: kbuf.at[i, :, heads], lambda i, h: kbuf.at[i, pl.ds(2 * h, 2), heads]
        )
        val = Ring(
            ys, y, lambda i: vbuf.at[:, i, heads], lambda i, h: vbuf.at[pl.ds(2 * h, 2), i, heads]
        )
        return key, val

    (key2a, val2a), (key2b, val2b) = pair_rings(pl.ds(0, 2)), pair_rings(pl.ds(2, 2))

    low64 = lax.broadcasted_iota(jnp.int32, (64, 128), 1) < 64
    for src, dst in ((pk_in, kbuf), (pv_in, vbuf)):
        for h in range(4):
            cut = slice(128 * (h // 2), 128 * (h // 2) + 128)
            pairs = []
            for g in (0, 2):
                a, b = src[g, :, cut].astype(F32), src[g + 1, :, cut].astype(F32)
                if h % 2 == 0:
                    pairs.append(jnp.where(low64, a, pltpu.roll(b, 64, 1)))
                else:
                    pairs.append(jnp.where(low64, pltpu.roll(a, 64, 1), b))
            dst[z, y, h] = jnp.concatenate(pairs, axis=1).astype(BF16)

    pl.semaphore_wait(barrier, len(peers))
    key1.start()
    val1.start()
    gate_a.start()
    up_a.start()
    down_a.start()
    over_k = send(k_in, zk, zs[1])
    over_v = send(v_in, zv, zs[1])

    first_row = di * 128
    group, start = token_info(
        len_in[...].astype(F32), grp_in[...].astype(F32), ord_in[...], first_row
    )
    lane_group = (lax.broadcasted_iota(jnp.int32, (128, 256), 1) // 64).astype(F32)
    in_group = (lane_group == group).astype(F32)
    window = (lax.broadcasted_iota(jnp.int32, (128, 256), 1) + (first_row - 128)).astype(F32)
    token = (lax.broadcasted_iota(jnp.int32, (128, 256), 0) + first_row).astype(F32)
    bias = jnp.where((window >= start) & (window <= token), 0.0, NEG_FILL)
    low = lax.broadcasted_iota(jnp.int32, (128, 128), 1) < 64

    def twice(block):
        turned = pltpu.roll(block, 64, 1)
        first, second = jnp.where(low, block, turned), jnp.where(low, turned, block)
        return jnp.concatenate([first, first], axis=1), jnp.concatenate([second, second], axis=1)

    def spread(src, dst, row):
        for b in (0, 1):
            first, second = twice(src[:, 128 * b:128 * b + 128].astype(F32))
            dst[2 * b, row:row + 128] = first.astype(BF16)
            dst[2 * b + 1, row:row + 128] = second.astype(BF16)

    key1.relay()
    val1.relay()
    up_a.relay1()
    up_b.start()

    over_k.wait_recv()
    over_v.wait_recv()
    edge = (y == 3).astype(F32)
    for src, over, staged in ((k_in, zk, sk), (v_in, zv, sv)):
        staged[...] = (
            over[...].astype(F32) * edge + src[...].astype(F32) * (1.0 - edge)
        ).astype(BF16)
    next_k = send(sk, kprev, ys[1])
    next_v = send(sv, vprev, ys[1])

    gate_a.relay1()
    down_a.relay1()
    key1.finish()
    key2a.start()
    key2b.start()
    up_a.finish1()
    up_a.turn()
    up_b.relay1()
    val1.finish()
    val2a.start()
    val2b.start()

    def spread_z(buf, lanes):
        return [
            send(buf.at[0, :, lanes], buf.at[3, :, lanes], zs[1]),
            send(buf.at[0, :, lanes], buf.at[1, :, lanes], zs[-1]),
        ]

    def onward(buf, copies, lanes):
        copies[0].wait_recv()
        a = send(buf.at[3, pl.ds(0, 64), lanes], buf.at[2, pl.ds(0, 64), lanes], zs[1])
        copies[1].wait_recv()
        b = send(buf.at[1, pl.ds(64, 64), lanes], buf.at[2, pl.ds(64, 64), lanes], zs[-1])
        return [a, b]

    res_lanes = [pl.ds(512 * n, 512) for n in range(4)]
    head_lanes = [pl.ds(256 * n, 256) for n in range(4)]
    local_res.wait()
    res_copies = [spread_z(res, res_lanes[0])]
    spread(k_in, ks, 128)
    spread(v_in, vs, 128)
    key2a.relay()
    up_b.finish1()
    up_b.turn()
    gate_a.finish1()
    key2b.relay()
    res_copies += [spread_z(res, lanes) for lanes in res_lanes[1:]]
    val2a.relay()
    up_a.relay2()
    val2b.relay()
    gate_b.start()
    down_b.start()
    next_k.wait_recv()
    next_v.wait_recv()
    spread(kprev, ks, 0)
    spread(vprev, vs, 0)
    key2a.finish()
    val2a.finish()

    bias4 = jnp.concatenate([bias] * 4, axis=0)
    in_group4 = jnp.concatenate([in_group] * 4, axis=0)

    def head(h):
        lanes = slice(256 * h, 256 * h + 256)
        block = q_in[:, lanes].astype(F32) * 0.125
        rows = [part * in_group for b in (0, 1) for part in twice(block[:, 128 * b:128 * b + 128])]
        qx = jnp.concatenate(rows, axis=0).astype(BF16)
        keys = kbuf[:, :, h].reshape(1024, 256)
        contract = (((1,), (1,)), ((), ()))
        s1 = lax.dot_general(qx, keys, contract, preferred_element_type=F32)
        s2 = lax.dot_general(qx, ks[h], contract, preferred_element_type=F32) + bias4
        peak = jnp.maximum(
            jnp.max(s1, axis=1, keepdims=True), jnp.max(s2, axis=1, keepdims=True)
        )
        p1, p2 = jnp.exp(s1 - peak), jnp.exp(s2 - peak)
        total = jnp.sum(p1, axis=1, keepdims=True) + jnp.sum(p2, axis=1, keepdims=True)
        o = jnp.dot(p1.astype(BF16), vbuf[:, :, h].reshape(1024, 256), preferred_element_type=F32)
        o = o + jnp.dot(p2.astype(BF16), vs[h], preferred_element_type=F32)
        o = o * in_group4
        o = o[:, :128] + o[:, 128:]
        o = (o + pltpu.roll(o, 64, 1)) * (1.0 / total)
        left, right = jnp.where(low, o[0:128], o[128:256]), jnp.where(low, o[256:384], o[384:512])
        attn[0, :, lanes] = jnp.concatenate([left, right], axis=1).astype(BF16)

    head(0)
    attn_copies = [spread_z(attn, head_lanes[0])]
    key2b.finish()
    val2b.finish()
    head(1)
    attn_copies.append(spread_z(attn, head_lanes[1]))
    up_b.relay2()
    arriving = [onward(res, res_copies[0], res_lanes[0])]
    arriving.append(onward(res, res_copies[1], res_lanes[1]))
    gate_b.relay1()
    gate_a.turn()
    head(2)
    attn_copies.append(spread_z(attn, head_lanes[2]))
    down_b.relay1()
    arriving.append(onward(attn, attn_copies[0], head_lanes[0]))
    gate_b.finish1()
    gate_b.turn()
    head(3)
    attn_copies.append(spread_z(attn, head_lanes[3]))
    arriving.append(onward(attn, attn_copies[1], head_lanes[1]))
    arriving.append(onward(res, res_copies[2], res_lanes[2]))
    arriving.append(onward(res, res_copies[3], res_lanes[3]))
    arriving.append(onward(attn, attn_copies[2], head_lanes[2]))
    up_a.finish2()
    down_a.finish1()
    last = onward(attn, attn_copies[3], head_lanes[3])
    up_b.finish2()
    local_out.wait()
    for copies in arriving:
        for copy in copies:
            copy.wait_recv()

    def project_first(n, carry):
        lanes = pl.ds(pl.multiple_of(n * 256, 256), 256)
        upv[n] = res[:, :, lanes].reshape(512, 256).astype(F32) + jnp.dot(
            attn[:, :, 0:768].reshape(512, 768), owb[0:768, lanes], preferred_element_type=F32
        )
        return carry

    lax.fori_loop(0, 8, project_first, 0)
    for copy in last:
        copy.wait_recv()

    def project(n, square):
        lanes = pl.ds(pl.multiple_of(n * 256, 256), 256)
        part = upv[n] + jnp.dot(
            attn[:, :, 768:1024].reshape(512, 256), owb[768:1024, lanes], preferred_element_type=F32
        )
        upv[n] = part
        hid[:, lanes] = part[0:128]
        return square + jnp.sum(part * part, axis=1, keepdims=True)

    square = lax.fori_loop(0, 8, project, jnp.zeros((512, 1), F32))
    gate_a.relay2()
    down_a.turn()
    scale = lax.rsqrt(square * (1.0 / 2048) + EPSILON)

    def normalize(n, carry):
        lanes = pl.ds(pl.multiple_of(n * 256, 256), 256)
        xn[:, lanes] = (upv[n] * scale * gain_in[:, lanes]).astype(BF16)
        return carry

    lax.fori_loop(0, 8, normalize, 0)
    down_b.finish1()
    gate_b.relay2()
    down_b.turn()
    up_a.ready()
    up_b.ready()

    def unit_columns(i):
        return i // 2, pl.ds(pl.multiple_of(lax.rem(i, 2) * 256, 256), 256)

    def up_units(i, carry):
        block, cols = unit_columns(i)
        upv[i] = jnp.dot(
            xn[...], wu[block, :, :, :, cols].reshape(2048, 256), preferred_element_type=F32
        )
        return carry

    lax.fori_loop(0, 8, up_units, 0)
    gate_a.finish2()
    gate_b.finish2()
    gate_a.ready()
    gate_b.ready()

    def gate_units(i, carry):
        block, cols = unit_columns(i)
        g = jnp.dot(
            xn[...], wg[block, :, :, :, cols].reshape(2048, 256), preferred_element_type=F32
        )
        act[:, pl.ds(pl.multiple_of(i * 256, 256), 256)] = (
            g / (1.0 + jnp.exp(-g)) * upv[i]
        ).astype(BF16)

        @pl.when(i == 5)
        def _():
            down_a.relay2()

        return carry

    lax.fori_loop(0, 8, gate_units, 0)
    down_b.ready(1)

    half0, half1 = pl.ds(0, 64), pl.ds(64, 64)
    first_hop = counter[0]
    counter[0] += 32

    def place(k):
        kind = 1 - lax.rem((k + 1) // 4, 2)
        i = lax.rem(x + k + k // 2, 4) * kind + (k - 3) * (1 - kind)
        return kind, i, kind * 4 + i

    def hop_copies(k):
        n = place(k)[2]
        return [
            pltpu.make_async_remote_copy(
                src_ref=src, dst_ref=dst, send_sem=ssem.at[first_hop + j * 8 + k],
                recv_sem=rsem.at[first_hop + j * 8 + k], device_id=device, device_id_type=MESH,
            )
            for j, (src, dst, device) in enumerate((
                (far.at[n, half0], hop.at[0, n], zs[1]),
                (far.at[n, half1], hop.at[1, n], zs[-1]),
                (near.at[0, n], back.at[0, n], zs[1]),
                (near.at[1, n], back.at[1, n], zs[-1]),
            ))
        ]

    def down_step(k, carry):
        @pl.when(k == 1)
        def _():
            down_b.relay2()
            down_b.ready(2)

        @pl.when(k == 3)
        def _():
            down_a.finish2()
            down_a.ready()

        @pl.when(k == 7)
        def _():
            down_b.finish2()
            down_b.ready()

        @pl.when(k < 8)
        def _():
            kind, i, n = place(k)
            weight = jnp.concatenate(
                [wd[kind, 0, i].reshape(2048, 128), wd[kind, 1, i].reshape(2048, 128)], axis=1
            )
            part = jnp.dot(act[...], weight, preferred_element_type=F32)
            far[n] = part[256:384].astype(BF16)
            copies = hop_copies(k)
            copies[0].start()
            copies[1].start()
            acc[n] = part[0:128]
            ends[0, n] = part[128:256]
            ends[1, n] = part[384:512]

        @pl.when(k > 0)
        def _():
            n = place(k - 1)[2]
            copies = hop_copies(k - 1)
            copies[0].wait_recv()
            near[0, n, 0:64] = (ends[0, n, 0:64] + hop[0, n].astype(F32)).astype(BF16)
            near[0, n, 64:128] = ends[0, n, 64:128].astype(BF16)
            copies[2].start()
            copies[1].wait_recv()
            near[1, n, 0:64] = ends[1, n, 0:64].astype(BF16)
            near[1, n, 64:128] = (ends[1, n, 64:128] + hop[1, n].astype(F32)).astype(BF16)
            copies[3].start()

        return carry

    lax.fori_loop(0, 9, down_step, 0)

    for k in range(8):
        copies = hop_copies(k)
        copies[2].wait_recv()
        copies[3].wait_recv()
        started.extend(copies)
    for half in range(2):
        for i in range(4):
            n = half * 4 + i
            total = acc[n] + back[0, n].astype(F32) + back[1, n].astype(F32)
            for cc in range(2):
                lanes = slice(512 * i + 256 * cc + 128 * half, 512 * i + 256 * cc + 128 * half + 128)
                out[:, lanes] = (hid[:, lanes] + total[:, 128 * cc:128 * cc + 128]).astype(BF16)

    for copy in started:
        copy.wait_send()
    assert counter[0] == N_SEM, counter[0]


def shards(
    residual, queries, keys, values, prefix_keys, cached_prefix_values, out_weight, norm_gain,
    w_gate, w_up, w_down, suffix_lengths, request_group, placement_order,
):
    vmem = pl.BlockSpec(memory_space=pltpu.VMEM)
    anywhere = pl.BlockSpec(memory_space=pl.ANY)
    return pl.pallas_call(
        kernel,
        out_shape=jax.ShapeDtypeStruct((128, 2048), BF16),
        in_specs=[
            anywhere, vmem, vmem, vmem, vmem, vmem, anywhere, vmem,
            anywhere, anywhere, anywhere, vmem, vmem, vmem,
        ],
        out_specs=vmem,
        scratch_shapes=[
            pltpu.VMEM((4, 4, 4, 64, 256), BF16),
            pltpu.VMEM((4, 4, 4, 64, 256), BF16),
            pltpu.VMEM((128, 256), BF16),
            pltpu.VMEM((128, 256), BF16),
            pltpu.VMEM((128, 256), BF16),
            pltpu.VMEM((128, 256), BF16),
            pltpu.VMEM((128, 256), BF16),
            pltpu.VMEM((128, 256), BF16),
            pltpu.VMEM((4, 256, 256), BF16),
            pltpu.VMEM((4, 256, 256), BF16),
            pltpu.VMEM((4, 128, 1024), BF16),
            pltpu.VMEM((1024, 2048), BF16),
            pltpu.VMEM((4, 128, 2048), BF16),
            pltpu.VMEM((128, 2048), F32),
            pltpu.VMEM((512, 2048), BF16),
            pltpu.VMEM((4, 4, 2, 256, 512), BF16),
            pltpu.VMEM((4, 4, 2, 256, 512), BF16),
            pltpu.VMEM((2, 2, 4, 4, 512, 128), BF16),
            pltpu.VMEM((8, 512, 256), F32),
            pltpu.VMEM((512, 2048), BF16),
            pltpu.VMEM((8, 128, 256), F32),
            pltpu.VMEM((2, 8, 128, 256), F32),
            pltpu.VMEM((8, 128, 256), BF16),
            pltpu.VMEM((2, 8, 64, 256), BF16),
            pltpu.VMEM((2, 8, 128, 256), BF16),
            pltpu.VMEM((2, 8, 128, 256), BF16),
            pltpu.SemaphoreType.DMA((N_SEM,)),
            pltpu.SemaphoreType.DMA((N_SEM,)),
            pltpu.SemaphoreType.DMA((6,)),
        ],
        compiler_params=pltpu.CompilerParams(
            collective_id=0, has_side_effects=True, vmem_limit_bytes=63 << 20
        ),
    )(
        residual, queries, keys, values, prefix_keys, cached_prefix_values, out_weight,
        norm_gain.reshape(1, -1), w_gate, w_up, w_down,
        suffix_lengths, request_group, placement_order,
    )


def solution(mesh):
    placed = (
        P(("grp", "dev"), None),
        P(("grp", "dev"), None),
        P(("grp", "dev"), None),
        P(("grp", "dev"), None),
        P("grp", "dev", None),
        P("grp", "dev", None),
        P(),
        P(),
        P("grp", "dev"),
        P("grp", "dev"),
        P("dev", "grp"),
        P("grp", None),
        P("grp", None),
        P("grp", None),
    )
    return jax.shard_map(
        shards, mesh=mesh, in_specs=placed, out_specs=P(("grp", "dev"), None), check_vma=False
    )
```

```python
import jax
import jax.numpy as jnp
from jax import lax
from jax.experimental import pallas as pl
from jax.experimental.pallas import tpu as pltpu
from jax.sharding import PartitionSpec as P

EPSILON = 1e-05
NEG_FILL = -1e30
MESH = pl.DeviceIdType.MESH
F32, BF16 = jnp.float32, jnp.bfloat16
N_SEM = 164


def token_info(lengths, groups, order, first_row):
    n = lengths.shape[1]
    rows = lax.broadcasted_iota(jnp.int32, (n, n), 0)
    cols = lax.broadcasted_iota(jnp.int32, (n, n), 1)
    diagonal = rows == cols

    def column(row):
        spread = jnp.broadcast_to(row, (n, n))
        return jnp.sum(jnp.where(diagonal, spread, 0.0), axis=1, keepdims=True)

    picked = jnp.broadcast_to(order, (n, n)) == rows
    packed_len = jnp.sum(jnp.where(picked, column(lengths), 0.0), axis=0, keepdims=True)
    packed_group = jnp.sum(jnp.where(picked, column(groups), 0.0), axis=0, keepdims=True)
    ends = jnp.sum(jnp.where(rows <= cols, column(packed_len), 0.0), axis=0, keepdims=True)
    starts = ends - packed_len
    token = (lax.broadcasted_iota(jnp.int32, (128, n), 0) + first_row).astype(F32)
    inside = (token >= starts) & (token < ends)
    group = jnp.sum(jnp.where(inside, packed_group, 0.0), axis=1, keepdims=True)
    start = jnp.sum(jnp.where(inside, starts, 0.0), axis=1, keepdims=True)
    return group, start


def kernel(
    res_in, q_in, k_in, v_in, pk_in, pv_in, ow_in, gain_in, wg_in, wu_in, wd_in, len_in, grp_in, ord_in,
    out,
    kbuf, vbuf, zk, zv, sk, sv, kprev, vprev, ks, vs, attn, owb, res, hid, xn, wg, wu, wd, upv, act,
    acc, ends, far, hop, near, back,
    ssem, rsem, lsem,
):
    gi, di = lax.axis_index("grp"), lax.axis_index("dev")
    x, c = gi // 2, lax.rem(gi, 2)
    z, y = di // 4, lax.rem(di, 4)

    def at(xx, cc, zz, yy):
        return (lax.rem(xx + 4, 4) * 2 + cc, lax.rem(zz + 4, 4) * 4 + lax.rem(yy + 4, 4))

    xs = {k: at(x + k, c, z, y) for k in (1, -1)}
    ys = {k: at(x, c, z, y + k) for k in (1, -1)}
    zs = {k: at(x, c, z + k, y) for k in (1, -1)}
    partner = (x * 2 + (1 - c), di)
    peers = [xs[1], xs[-1], ys[1], ys[-1], zs[1], zs[-1], partner]

    barrier = pltpu.get_barrier_semaphore()
    for peer in peers:
        pl.semaphore_signal(barrier, inc=1, device_id=peer, device_id_type=MESH)

    started = []
    counter = [0]

    class Copy:
        def __init__(self, src, dst, device, i):
            self.src, self.dst, self.device, self.i = src, dst, device, i

        def copy(self):
            src, dst = [ref() if callable(ref) else ref for ref in (self.src, self.dst)]
            return pltpu.make_async_remote_copy(
                src_ref=src, dst_ref=dst, send_sem=ssem.at[self.i], recv_sem=rsem.at[self.i],
                device_id=self.device, device_id_type=MESH,
            )

        def start(self):
            self.copy().start()

        def wait_recv(self):
            self.copy().wait_recv()

        def wait_send(self):
            self.copy().wait_send()

    def send(src, dst, device):
        copy = Copy(src, dst, device, counter[0])
        counter[0] += 1
        copy.start()
        started.append(copy)
        return copy

    local_count = [0]

    def bring(src, dst):
        i = local_count[0]
        local_count[0] += 1
        copy = pltpu.make_async_copy(src, dst, lsem.at[i])
        copy.start()
        return copy

    class Ring:
        def __init__(self, where, pos, slot, half):
            self.where, self.pos, self.slot, self.half = where, pos, slot, half
            self.before, self.after, self.far = [lax.rem(pos + k, 4) for k in (3, 1, 2)]

        def start(self, src=None):
            mine = lambda: self.slot(self.pos)
            src = mine if src is None else src
            self.up = send(src, mine, self.where[1])
            self.down = send(src, mine, self.where[-1])

        def relay(self):
            before, after = self.before, self.after
            self.up.wait_recv()
            first, second = lambda: self.half(before, 0), lambda: self.half(after, 1)
            self.a = send(first, first, self.where[1])
            self.down.wait_recv()
            self.b = send(second, second, self.where[-1])

        def finish(self):
            self.a.wait_recv()
            self.b.wait_recv()

        def around(self):
            return [self.before, self.after, self.far]

    class Piece:
        def __init__(self, first, second, src, local):
            self.first, self.second, self.src, self.local = first, second, src, local
            self.shared = []

        def share(self, i):
            block = lambda: self.second.slot(i)
            self.shared.append(send(block, block, partner))

        def start(self):
            self.first.start(self.src)

        def relay1(self):
            self.first.relay()

        def finish1(self):
            self.first.finish()
            if self.local is not None:
                self.local.wait()
            self.share(self.second.pos)

        def turn(self):
            self.second.start()

        def relay2(self):
            self.second.relay()
            for i in self.second.around()[:2]:
                self.share(i)

        def finish2(self):
            self.second.finish()
            self.share(self.second.around()[2])

        def ready(self, n=None):
            for copy in self.shared[:n] if n is not None else self.shared:
                copy.wait_recv()
            self.shared = self.shared[n:] if n is not None else []

    local_gate = bring(wg_in, wg.at[y, x, c])
    local_up = bring(wu_in, wu.at[y, x, c])
    local_da = bring(wd_in.at[:, pl.ds(0, 128)], wd.at[0, c, x, y])
    local_db = bring(wd_in.at[:, pl.ds(128, 128)], wd.at[1, c, x, y])
    local_res = bring(res_in, res.at[0])
    local_out = bring(ow_in, owb)

    top, bottom = pl.ds(0, 128), pl.ds(128, 128)

    def quarter(lo, h):
        return pl.ds(lo + 64 * h, 64)

    gate_a = Piece(
        Ring(xs, x, lambda i: wg.at[y, i, c, top], lambda i, h: wg.at[y, i, c, quarter(0, h)]),
        Ring(ys, y, lambda i: wg.at[i, :, c, top], lambda i, h: wg.at[i, pl.ds(2 * h, 2), c, top]),
        wg_in.at[top], local_gate,
    )
    gate_b = Piece(
        Ring(ys, y, lambda i: wg.at[i, x, c, bottom], lambda i, h: wg.at[i, x, c, quarter(128, h)]),
        Ring(xs, x, lambda i: wg.at[:, i, c, bottom], lambda i, h: wg.at[pl.ds(2 * h, 2), i, c, bottom]),
        wg_in.at[bottom], None,
    )
    up_a = Piece(
        Ring(ys, y, lambda i: wu.at[i, x, c, top], lambda i, h: wu.at[i, x, c, quarter(0, h)]),
        Ring(xs, x, lambda i: wu.at[:, i, c, top], lambda i, h: wu.at[pl.ds(2 * h, 2), i, c, top]),
        wu_in.at[top], local_up,
    )
    up_b = Piece(
        Ring(ys, y, lambda i: wu.at[i, x, c, bottom], lambda i, h: wu.at[i, x, c, quarter(128, h)]),
        Ring(xs, x, lambda i: wu.at[:, i, c, bottom], lambda i, h: wu.at[pl.ds(2 * h, 2), i, c, bottom]),
        wu_in.at[bottom], None,
    )
    down_a = Piece(
        Ring(xs, x, lambda i: wd.at[0, c, i, y], lambda i, h: wd.at[0, c, i, y, pl.ds(256 * h, 256)]),
        Ring(ys, y, lambda i: wd.at[0, c, :, i], lambda i, h: wd.at[0, c, pl.ds(2 * h, 2), i]),
        wd_in.at[:, pl.ds(0, 128)], local_da,
    )
    down_b = Piece(
        Ring(ys, y, lambda i: wd.at[1, c, x, i], lambda i, h: wd.at[1, c, x, i, pl.ds(256 * h, 256)]),
        Ring(xs, x, lambda i: wd.at[1, c, i], lambda i, h: wd.at[1, c, i, pl.ds(2 * h, 2)]),
        wd_in.at[:, pl.ds(128, 128)], local_db,
    )
    key1 = Ring(ys, y, lambda i: kbuf.at[z, i], lambda i, h: kbuf.at[z, i, pl.ds(2 * h, 2)])
    val1 = Ring(zs, z, lambda i: vbuf.at[i, y], lambda i, h: vbuf.at[i, y, pl.ds(2 * h, 2)])

    def pair_rings(heads):
        key = Ring(
            zs, z, lambda i: kbuf.at[i, :, heads], lambda i, h: kbuf.at[i, pl.ds(2 * h, 2), heads]
        )
        val = Ring(
            ys, y, lambda i: vbuf.at[:, i, heads], lambda i, h: vbuf.at[pl.ds(2 * h, 2), i, heads]
        )
        return key, val

    (key2a, val2a), (key2b, val2b) = pair_rings(pl.ds(0, 2)), pair_rings(pl.ds(2, 2))

    low64 = lax.broadcasted_iota(jnp.int32, (64, 128), 1) < 64
    for src, dst in ((pk_in, kbuf), (pv_in, vbuf)):
        for h in range(4):
            cut = slice(128 * (h // 2), 128 * (h // 2) + 128)
            pairs = []
            for g in (0, 2):
                a, b = src[g, :, cut].astype(F32), src[g + 1, :, cut].astype(F32)
                if h % 2 == 0:
                    pairs.append(jnp.where(low64, a, pltpu.roll(b, 64, 1)))
                else:
                    pairs.append(jnp.where(low64, pltpu.roll(a, 64, 1), b))
            dst[z, y, h] = jnp.concatenate(pairs, axis=1).astype(BF16)

    pl.semaphore_wait(barrier, len(peers))
    key1.start()
    val1.start()
    gate_a.start()
    up_a.start()
    down_a.start()
    over_k = send(k_in, zk, zs[1])
    over_v = send(v_in, zv, zs[1])

    first_row = di * 128
    group, start = token_info(
        len_in[...].astype(F32), grp_in[...].astype(F32), ord_in[...], first_row
    )
    lane_group = (lax.broadcasted_iota(jnp.int32, (128, 256), 1) // 64).astype(F32)
    in_group = (lane_group == group).astype(F32)
    window = (lax.broadcasted_iota(jnp.int32, (128, 256), 1) + (first_row - 128)).astype(F32)
    token = (lax.broadcasted_iota(jnp.int32, (128, 256), 0) + first_row).astype(F32)
    bias = jnp.where((window >= start) & (window <= token), 0.0, NEG_FILL)
    low = lax.broadcasted_iota(jnp.int32, (128, 128), 1) < 64

    def twice(block):
        turned = pltpu.roll(block, 64, 1)
        first, second = jnp.where(low, block, turned), jnp.where(low, turned, block)
        return jnp.concatenate([first, first], axis=1), jnp.concatenate([second, second], axis=1)

    def spread(src, dst, row):
        for b in (0, 1):
            first, second = twice(src[:, 128 * b:128 * b + 128].astype(F32))
            dst[2 * b, row:row + 128] = first.astype(BF16)
            dst[2 * b + 1, row:row + 128] = second.astype(BF16)

    key1.relay()
    val1.relay()
    up_a.relay1()
    up_b.start()

    over_k.wait_recv()
    over_v.wait_recv()
    edge = (y == 3).astype(F32)
    for src, over, staged in ((k_in, zk, sk), (v_in, zv, sv)):
        staged[...] = (
            over[...].astype(F32) * edge + src[...].astype(F32) * (1.0 - edge)
        ).astype(BF16)
    next_k = send(sk, kprev, ys[1])
    next_v = send(sv, vprev, ys[1])

    gate_a.relay1()
    down_a.relay1()
    key1.finish()
    key2a.start()
    key2b.start()
    up_a.finish1()
    up_a.turn()
    up_b.relay1()
    val1.finish()
    val2a.start()
    val2b.start()

    def spread_z(buf, lanes):
        return [
            send(buf.at[0, :, lanes], buf.at[3, :, lanes], zs[1]),
            send(buf.at[0, :, lanes], buf.at[1, :, lanes], zs[-1]),
        ]

    def onward(buf, copies, lanes):
        copies[0].wait_recv()
        a = send(buf.at[3, pl.ds(0, 64), lanes], buf.at[2, pl.ds(0, 64), lanes], zs[1])
        copies[1].wait_recv()
        b = send(buf.at[1, pl.ds(64, 64), lanes], buf.at[2, pl.ds(64, 64), lanes], zs[-1])
        return [a, b]

    res_lanes = [pl.ds(512 * n, 512) for n in range(4)]
    head_lanes = [pl.ds(256 * n, 256) for n in range(4)]
    local_res.wait()
    res_copies = [spread_z(res, res_lanes[0])]
    spread(k_in, ks, 128)
    spread(v_in, vs, 128)
    key2a.relay()
    up_b.finish1()
    up_b.turn()
    gate_a.finish1()
    key2b.relay()
    res_copies += [spread_z(res, lanes) for lanes in res_lanes[1:]]
    val2a.relay()
    up_a.relay2()
    val2b.relay()
    gate_b.start()
    down_b.start()
    next_k.wait_recv()
    next_v.wait_recv()
    spread(kprev, ks, 0)
    spread(vprev, vs, 0)
    key2a.finish()
    val2a.finish()

    bias4 = jnp.concatenate([bias] * 4, axis=0)
    in_group4 = jnp.concatenate([in_group] * 4, axis=0)

    def head(h):
        lanes = slice(256 * h, 256 * h + 256)
        block = q_in[:, lanes].astype(F32) * 0.125
        rows = [part * in_group for b in (0, 1) for part in twice(block[:, 128 * b:128 * b + 128])]
        qx = jnp.concatenate(rows, axis=0).astype(BF16)
        keys = kbuf[:, :, h].reshape(1024, 256)
        contract = (((1,), (1,)), ((), ()))
        s1 = lax.dot_general(qx, keys, contract, preferred_element_type=F32)
        s2 = lax.dot_general(qx, ks[h], contract, preferred_element_type=F32) + bias4
        peak = jnp.maximum(
            jnp.max(s1, axis=1, keepdims=True), jnp.max(s2, axis=1, keepdims=True)
        )
        p1, p2 = jnp.exp(s1 - peak), jnp.exp(s2 - peak)
        total = jnp.sum(p1, axis=1, keepdims=True) + jnp.sum(p2, axis=1, keepdims=True)
        o = jnp.dot(p1.astype(BF16), vbuf[:, :, h].reshape(1024, 256), preferred_element_type=F32)
        o = o + jnp.dot(p2.astype(BF16), vs[h], preferred_element_type=F32)
        o = o * in_group4
        o = o[:, :128] + o[:, 128:]
        o = (o + pltpu.roll(o, 64, 1)) * (1.0 / total)
        left, right = jnp.where(low, o[0:128], o[128:256]), jnp.where(low, o[256:384], o[384:512])
        attn[0, :, lanes] = jnp.concatenate([left, right], axis=1).astype(BF16)

    head(0)
    attn_copies = [spread_z(attn, head_lanes[0])]
    key2b.finish()
    val2b.finish()
    head(1)
    attn_copies.append(spread_z(attn, head_lanes[1]))
    up_b.relay2()
    arriving = [onward(res, res_copies[0], res_lanes[0])]
    arriving.append(onward(res, res_copies[1], res_lanes[1]))
    gate_b.relay1()
    head(2)
    attn_copies.append(spread_z(attn, head_lanes[2]))
    down_b.relay1()
    gate_a.turn()
    arriving.append(onward(attn, attn_copies[0], head_lanes[0]))
    gate_b.finish1()
    gate_b.turn()
    head(3)
    attn_copies.append(spread_z(attn, head_lanes[3]))
    arriving.append(onward(attn, attn_copies[1], head_lanes[1]))
    arriving.append(onward(res, res_copies[2], res_lanes[2]))
    arriving.append(onward(res, res_copies[3], res_lanes[3]))
    arriving.append(onward(attn, attn_copies[2], head_lanes[2]))
    up_a.finish2()
    down_a.finish1()
    last = onward(attn, attn_copies[3], head_lanes[3])
    up_b.finish2()
    local_out.wait()
    for copies in arriving:
        for copy in copies:
            copy.wait_recv()

    down_b.finish1()

    def project_first(n, carry):
        lanes = pl.ds(pl.multiple_of(n * 256, 256), 256)
        upv[n] = res[:, :, lanes].reshape(512, 256).astype(F32) + jnp.dot(
            attn[:, :, 0:768].reshape(512, 768), owb[0:768, lanes], preferred_element_type=F32
        )

        @pl.when(n == 4)
        def _():
            gate_a.relay2()
            down_a.turn()

        @pl.when(n == 7)
        def _():
            gate_b.relay2()
            down_b.turn()

        return carry

    lax.fori_loop(0, 8, project_first, 0)
    for copy in last:
        copy.wait_recv()

    def project(n, square):
        lanes = pl.ds(pl.multiple_of(n * 256, 256), 256)
        part = upv[n] + jnp.dot(
            attn[:, :, 768:1024].reshape(512, 256), owb[768:1024, lanes], preferred_element_type=F32
        )
        upv[n] = part
        hid[:, lanes] = part[0:128]
        return square + jnp.sum(part * part, axis=1, keepdims=True)

    square = lax.fori_loop(0, 8, project, jnp.zeros((512, 1), F32))
    scale = lax.rsqrt(square * (1.0 / 2048) + EPSILON)

    def normalize(n, carry):
        lanes = pl.ds(pl.multiple_of(n * 256, 256), 256)
        xn[:, lanes] = (upv[n] * scale * gain_in[:, lanes]).astype(BF16)
        return carry

    lax.fori_loop(0, 8, normalize, 0)
    up_a.ready()
    up_b.ready()

    def unit_columns(i):
        return i // 2, pl.ds(pl.multiple_of(lax.rem(i, 2) * 256, 256), 256)

    def up_units(i, carry):
        block, cols = unit_columns(i)
        upv[i] = jnp.dot(
            xn[...], wu[block, :, :, :, cols].reshape(2048, 256), preferred_element_type=F32
        )

        @pl.when(i == 3)
        def _():
            gate_a.finish2()

        @pl.when(i == 5)
        def _():
            gate_b.finish2()

        return carry

    lax.fori_loop(0, 8, up_units, 0)
    gate_a.ready()
    gate_b.ready()

    def gate_units(i, carry):
        block, cols = unit_columns(i)
        g = jnp.dot(
            xn[...], wg[block, :, :, :, cols].reshape(2048, 256), preferred_element_type=F32
        )
        act[:, pl.ds(pl.multiple_of(i * 256, 256), 256)] = (
            g / (1.0 + jnp.exp(-g)) * upv[i]
        ).astype(BF16)

        @pl.when(i == 4)
        def _():
            down_a.relay2()

        return carry

    lax.fori_loop(0, 8, gate_units, 0)
    down_b.ready(1)

    half0, half1 = pl.ds(0, 64), pl.ds(64, 64)
    first_hop = counter[0]
    counter[0] += 32

    def place(k):
        kind = 1 - lax.rem((k + 1) // 4, 2)
        i = lax.rem(x + k + k // 2, 4) * kind + (k - 3) * (1 - kind)
        return kind, i, kind * 4 + i

    def hop_copies(k):
        n = place(k)[2]
        return [
            pltpu.make_async_remote_copy(
                src_ref=src, dst_ref=dst, send_sem=ssem.at[first_hop + j * 8 + k],
                recv_sem=rsem.at[first_hop + j * 8 + k], device_id=device, device_id_type=MESH,
            )
            for j, (src, dst, device) in enumerate((
                (far.at[n, half0], hop.at[0, n], zs[1]),
                (far.at[n, half1], hop.at[1, n], zs[-1]),
                (near.at[0, n], back.at[0, n], zs[1]),
                (near.at[1, n], back.at[1, n], zs[-1]),
            ))
        ]

    def pass_on(k):
        n = place(k)[2]
        copies = hop_copies(k)
        copies[0].wait_recv()
        near[0, n, 0:64] = (ends[0, n, 0:64] + hop[0, n].astype(F32)).astype(BF16)
        near[0, n, 64:128] = ends[0, n, 64:128].astype(BF16)
        copies[2].start()
        copies[1].wait_recv()
        near[1, n, 0:64] = ends[1, n, 0:64].astype(BF16)
        near[1, n, 64:128] = (ends[1, n, 64:128] + hop[1, n].astype(F32)).astype(BF16)
        copies[3].start()

    def down_step(k, carry):
        @pl.when(k == 1)
        def _():
            down_b.relay2()
            pass_on(0)
            down_b.ready(2)

        @pl.when(k == 2)
        def _():
            down_a.finish2()

        @pl.when(k == 3)
        def _():
            down_a.ready()

        @pl.when(k == 4)
        def _():
            down_b.finish2()

        @pl.when(k == 7)
        def _():
            down_b.ready()

        @pl.when(k < 8)
        def _():
            kind, i, n = place(k)
            weight = jnp.concatenate(
                [wd[kind, 0, i].reshape(2048, 128), wd[kind, 1, i].reshape(2048, 128)], axis=1
            )
            part = jnp.dot(act[...], weight, preferred_element_type=F32)
            far[n] = part[256:384].astype(BF16)
            copies = hop_copies(k)
            copies[0].start()
            copies[1].start()
            acc[n] = part[0:128]
            ends[0, n] = part[128:256]
            ends[1, n] = part[384:512]

        @pl.when(k > 2)
        def _():
            pass_on(k - 2)

        return carry

    lax.fori_loop(0, 10, down_step, 0)

    def collect(k, carry):
        copies = hop_copies(k)
        copies[2].wait_recv()
        copies[3].wait_recv()
        kind, i, n = place(k)
        total = acc[n] + back[0, n].astype(F32) + back[1, n].astype(F32)
        for cc in range(2):
            lanes = pl.ds(pl.multiple_of(512 * i + 256 * cc + 128 * kind, 128), 128)
            out[:, lanes] = (hid[:, lanes] + total[:, 128 * cc:128 * cc + 128]).astype(BF16)
        return carry

    lax.fori_loop(0, 8, collect, 0)
    for k in range(8):
        started.extend(hop_copies(k))

    for copy in started:
        copy.wait_send()
    assert counter[0] == N_SEM, counter[0]


def shards(
    residual, queries, keys, values, prefix_keys, cached_prefix_values, out_weight, norm_gain,
    w_gate, w_up, w_down, suffix_lengths, request_group, placement_order,
):
    vmem = pl.BlockSpec(memory_space=pltpu.VMEM)
    anywhere = pl.BlockSpec(memory_space=pl.ANY)
    return pl.pallas_call(
        kernel,
        out_shape=jax.ShapeDtypeStruct((128, 2048), BF16),
        in_specs=[
            anywhere, vmem, vmem, vmem, vmem, vmem, anywhere, vmem,
            anywhere, anywhere, anywhere, vmem, vmem, vmem,
        ],
        out_specs=vmem,
        scratch_shapes=[
            pltpu.VMEM((4, 4, 4, 64, 256), BF16),
            pltpu.VMEM((4, 4, 4, 64, 256), BF16),
            pltpu.VMEM((128, 256), BF16),
            pltpu.VMEM((128, 256), BF16),
            pltpu.VMEM((128, 256), BF16),
            pltpu.VMEM((128, 256), BF16),
            pltpu.VMEM((128, 256), BF16),
            pltpu.VMEM((128, 256), BF16),
            pltpu.VMEM((4, 256, 256), BF16),
            pltpu.VMEM((4, 256, 256), BF16),
            pltpu.VMEM((4, 128, 1024), BF16),
            pltpu.VMEM((1024, 2048), BF16),
            pltpu.VMEM((4, 128, 2048), BF16),
            pltpu.VMEM((128, 2048), F32),
            pltpu.VMEM((512, 2048), BF16),
            pltpu.VMEM((4, 4, 2, 256, 512), BF16),
            pltpu.VMEM((4, 4, 2, 256, 512), BF16),
            pltpu.VMEM((2, 2, 4, 4, 512, 128), BF16),
            pltpu.VMEM((8, 512, 256), F32),
            pltpu.VMEM((512, 2048), BF16),
            pltpu.VMEM((8, 128, 256), F32),
            pltpu.VMEM((2, 8, 128, 256), F32),
            pltpu.VMEM((8, 128, 256), BF16),
            pltpu.VMEM((2, 8, 64, 256), BF16),
            pltpu.VMEM((2, 8, 128, 256), BF16),
            pltpu.VMEM((2, 8, 128, 256), BF16),
            pltpu.SemaphoreType.DMA((N_SEM,)),
            pltpu.SemaphoreType.DMA((N_SEM,)),
            pltpu.SemaphoreType.DMA((6,)),
        ],
        compiler_params=pltpu.CompilerParams(
            collective_id=0, has_side_effects=True, vmem_limit_bytes=63 << 20
        ),
    )(
        residual, queries, keys, values, prefix_keys, cached_prefix_values, out_weight,
        norm_gain.reshape(1, -1), w_gate, w_up, w_down,
        suffix_lengths, request_group, placement_order,
    )


def solution(mesh):
    placed = (
        P(("grp", "dev"), None),
        P(("grp", "dev"), None),
        P(("grp", "dev"), None),
        P(("grp", "dev"), None),
        P("grp", "dev", None),
        P("grp", "dev", None),
        P(),
        P(),
        P("grp", "dev"),
        P("grp", "dev"),
        P("dev", "grp"),
        P("grp", None),
        P("grp", None),
        P("grp", None),
    )
    return jax.shard_map(
        shards, mesh=mesh, in_specs=placed, out_specs=P(("grp", "dev"), None), check_vma=False
    )
```

```python
import jax
import jax.numpy as jnp
from jax import lax
from jax.experimental import pallas as pl
from jax.experimental.pallas import tpu as pltpu
from jax.sharding import PartitionSpec as P

EPSILON = 1e-05
NEG_FILL = -1e30
MESH = pl.DeviceIdType.MESH
F32, BF16 = jnp.float32, jnp.bfloat16
N_SEM = 164


def token_info(lengths, groups, order, first_row):
    n = lengths.shape[1]
    rows = lax.broadcasted_iota(jnp.int32, (n, n), 0)
    cols = lax.broadcasted_iota(jnp.int32, (n, n), 1)
    diagonal = rows == cols

    def column(row):
        spread = jnp.broadcast_to(row, (n, n))
        return jnp.sum(jnp.where(diagonal, spread, 0.0), axis=1, keepdims=True)

    picked = jnp.broadcast_to(order, (n, n)) == rows
    packed_len = jnp.sum(jnp.where(picked, column(lengths), 0.0), axis=0, keepdims=True)
    packed_group = jnp.sum(jnp.where(picked, column(groups), 0.0), axis=0, keepdims=True)
    ends = jnp.sum(jnp.where(rows <= cols, column(packed_len), 0.0), axis=0, keepdims=True)
    starts = ends - packed_len
    token = (lax.broadcasted_iota(jnp.int32, (128, n), 0) + first_row).astype(F32)
    inside = (token >= starts) & (token < ends)
    group = jnp.sum(jnp.where(inside, packed_group, 0.0), axis=1, keepdims=True)
    start = jnp.sum(jnp.where(inside, starts, 0.0), axis=1, keepdims=True)
    return group, start


def kernel(
    res_in, q_in, k_in, v_in, pk_in, pv_in, ow_in, gain_in, wg_in, wu_in, wd_in, len_in, grp_in, ord_in,
    out,
    kbuf, vbuf, zk, zv, sk, sv, kprev, vprev, ks, vs, attn, owb, res, hid, xn, wg, wu, wd, upv, act,
    acc, ends, far, hop, near, back,
    ssem, rsem, lsem,
):
    gi, di = lax.axis_index("grp"), lax.axis_index("dev")
    x, c = gi // 2, lax.rem(gi, 2)
    z, y = di // 4, lax.rem(di, 4)

    def at(xx, cc, zz, yy):
        return (lax.rem(xx + 4, 4) * 2 + cc, lax.rem(zz + 4, 4) * 4 + lax.rem(yy + 4, 4))

    xs = {k: at(x + k, c, z, y) for k in (1, -1)}
    ys = {k: at(x, c, z, y + k) for k in (1, -1)}
    zs = {k: at(x, c, z + k, y) for k in (1, -1)}
    partner = (x * 2 + (1 - c), di)
    peers = [xs[1], xs[-1], ys[1], ys[-1], zs[1], zs[-1], partner]

    barrier = pltpu.get_barrier_semaphore()
    for peer in peers:
        pl.semaphore_signal(barrier, inc=1, device_id=peer, device_id_type=MESH)

    started = []
    counter = [0]

    class Copy:
        def __init__(self, src, dst, device, i):
            self.src, self.dst, self.device, self.i = src, dst, device, i

        def copy(self):
            src, dst = [ref() if callable(ref) else ref for ref in (self.src, self.dst)]
            return pltpu.make_async_remote_copy(
                src_ref=src, dst_ref=dst, send_sem=ssem.at[self.i], recv_sem=rsem.at[self.i],
                device_id=self.device, device_id_type=MESH,
            )

        def start(self):
            self.copy().start()

        def wait_recv(self):
            self.copy().wait_recv()

        def wait_send(self):
            self.copy().wait_send()

    def send(src, dst, device):
        copy = Copy(src, dst, device, counter[0])
        counter[0] += 1
        copy.start()
        started.append(copy)
        return copy

    local_count = [0]

    def bring(src, dst):
        i = local_count[0]
        local_count[0] += 1
        copy = pltpu.make_async_copy(src, dst, lsem.at[i])
        copy.start()
        return copy

    class Ring:
        def __init__(self, where, pos, slot, half):
            self.where, self.pos, self.slot, self.half = where, pos, slot, half
            self.before, self.after, self.far = [lax.rem(pos + k, 4) for k in (3, 1, 2)]

        def start(self, src=None):
            mine = lambda: self.slot(self.pos)
            src = mine if src is None else src
            self.up = send(src, mine, self.where[1])
            self.down = send(src, mine, self.where[-1])

        def relay(self):
            before, after = self.before, self.after
            self.up.wait_recv()
            first, second = lambda: self.half(before, 0), lambda: self.half(after, 1)
            self.a = send(first, first, self.where[1])
            self.down.wait_recv()
            self.b = send(second, second, self.where[-1])

        def finish(self):
            self.a.wait_recv()
            self.b.wait_recv()

        def around(self):
            return [self.before, self.after, self.far]

    class Piece:
        def __init__(self, first, second, src, local):
            self.first, self.second, self.src, self.local = first, second, src, local
            self.shared = []

        def share(self, i):
            block = lambda: self.second.slot(i)
            self.shared.append(send(block, block, partner))

        def start(self):
            self.first.start(self.src)

        def relay1(self):
            self.first.relay()

        def finish1(self):
            self.first.finish()
            if self.local is not None:
                self.local.wait()
            self.share(self.second.pos)

        def turn(self):
            self.second.start()

        def relay2(self):
            self.second.relay()
            for i in self.second.around()[:2]:
                self.share(i)

        def finish2(self):
            self.second.finish()
            self.share(self.second.around()[2])

        def ready(self, n=None):
            for copy in self.shared[:n] if n is not None else self.shared:
                copy.wait_recv()
            self.shared = self.shared[n:] if n is not None else []

    local_gate = bring(wg_in, wg.at[y, x, c])
    local_up = bring(wu_in, wu.at[y, x, c])
    local_da = bring(wd_in.at[:, pl.ds(0, 128)], wd.at[0, c, x, y])
    local_db = bring(wd_in.at[:, pl.ds(128, 128)], wd.at[1, c, x, y])
    local_res = bring(res_in, res.at[0])
    local_out = bring(ow_in, owb)

    top, bottom = pl.ds(0, 128), pl.ds(128, 128)

    def quarter(lo, h):
        return pl.ds(lo + 64 * h, 64)

    more, less = pl.ds(0, 144), pl.ds(144, 112)
    gate_a = Piece(
        Ring(xs, x, lambda i: wg.at[y, i, c, more], lambda i, h: wg.at[y, i, c, (pl.ds(0, 80), pl.ds(80, 64))[h]]),
        Ring(ys, y, lambda i: wg.at[i, :, c, more], lambda i, h: wg.at[i, pl.ds(2 * h, 2), c, more]),
        wg_in.at[more], local_gate,
    )
    gate_b = Piece(
        Ring(ys, y, lambda i: wg.at[i, x, c, less], lambda i, h: wg.at[i, x, c, (pl.ds(144, 64), pl.ds(208, 48))[h]]),
        Ring(xs, x, lambda i: wg.at[:, i, c, less], lambda i, h: wg.at[pl.ds(2 * h, 2), i, c, less]),
        wg_in.at[less], None,
    )
    up_a = Piece(
        Ring(ys, y, lambda i: wu.at[i, x, c, top], lambda i, h: wu.at[i, x, c, quarter(0, h)]),
        Ring(xs, x, lambda i: wu.at[:, i, c, top], lambda i, h: wu.at[pl.ds(2 * h, 2), i, c, top]),
        wu_in.at[top], local_up,
    )
    up_b = Piece(
        Ring(ys, y, lambda i: wu.at[i, x, c, bottom], lambda i, h: wu.at[i, x, c, quarter(128, h)]),
        Ring(xs, x, lambda i: wu.at[:, i, c, bottom], lambda i, h: wu.at[pl.ds(2 * h, 2), i, c, bottom]),
        wu_in.at[bottom], None,
    )
    down_a = Piece(
        Ring(xs, x, lambda i: wd.at[0, c, i, y], lambda i, h: wd.at[0, c, i, y, pl.ds(256 * h, 256)]),
        Ring(ys, y, lambda i: wd.at[0, c, :, i], lambda i, h: wd.at[0, c, pl.ds(2 * h, 2), i]),
        wd_in.at[:, pl.ds(0, 128)], local_da,
    )
    down_b = Piece(
        Ring(ys, y, lambda i: wd.at[1, c, x, i], lambda i, h: wd.at[1, c, x, i, pl.ds(256 * h, 256)]),
        Ring(xs, x, lambda i: wd.at[1, c, i], lambda i, h: wd.at[1, c, i, pl.ds(2 * h, 2)]),
        wd_in.at[:, pl.ds(128, 128)], local_db,
    )
    key1 = Ring(ys, y, lambda i: kbuf.at[z, i], lambda i, h: kbuf.at[z, i, pl.ds(2 * h, 2)])
    val1 = Ring(zs, z, lambda i: vbuf.at[i, y], lambda i, h: vbuf.at[i, y, pl.ds(2 * h, 2)])

    def pair_rings(heads):
        key = Ring(
            zs, z, lambda i: kbuf.at[i, :, heads], lambda i, h: kbuf.at[i, pl.ds(2 * h, 2), heads]
        )
        val = Ring(
            ys, y, lambda i: vbuf.at[:, i, heads], lambda i, h: vbuf.at[pl.ds(2 * h, 2), i, heads]
        )
        return key, val

    (key2a, val2a), (key2b, val2b) = pair_rings(pl.ds(0, 2)), pair_rings(pl.ds(2, 2))

    low64 = lax.broadcasted_iota(jnp.int32, (64, 128), 1) < 64
    for src, dst in ((pk_in, kbuf), (pv_in, vbuf)):
        for h in range(4):
            cut = slice(128 * (h // 2), 128 * (h // 2) + 128)
            pairs = []
            for g in (0, 2):
                a, b = src[g, :, cut].astype(F32), src[g + 1, :, cut].astype(F32)
                if h % 2 == 0:
                    pairs.append(jnp.where(low64, a, pltpu.roll(b, 64, 1)))
                else:
                    pairs.append(jnp.where(low64, pltpu.roll(a, 64, 1), b))
            dst[z, y, h] = jnp.concatenate(pairs, axis=1).astype(BF16)

    pl.semaphore_wait(barrier, len(peers))
    key1.start()
    val1.start()
    gate_a.start()
    up_a.start()
    down_a.start()
    over_k = send(k_in, zk, zs[1])
    over_v = send(v_in, zv, zs[1])

    first_row = di * 128
    group, start = token_info(
        len_in[...].astype(F32), grp_in[...].astype(F32), ord_in[...], first_row
    )
    lane_group = (lax.broadcasted_iota(jnp.int32, (128, 256), 1) // 64).astype(F32)
    in_group = (lane_group == group).astype(F32)
    window = (lax.broadcasted_iota(jnp.int32, (128, 256), 1) + (first_row - 128)).astype(F32)
    token = (lax.broadcasted_iota(jnp.int32, (128, 256), 0) + first_row).astype(F32)
    bias = jnp.where((window >= start) & (window <= token), 0.0, NEG_FILL)
    low = lax.broadcasted_iota(jnp.int32, (128, 128), 1) < 64

    def twice(block):
        turned = pltpu.roll(block, 64, 1)
        first, second = jnp.where(low, block, turned), jnp.where(low, turned, block)
        return jnp.concatenate([first, first], axis=1), jnp.concatenate([second, second], axis=1)

    def spread(src, dst, row):
        for b in (0, 1):
            first, second = twice(src[:, 128 * b:128 * b + 128].astype(F32))
            dst[2 * b, row:row + 128] = first.astype(BF16)
            dst[2 * b + 1, row:row + 128] = second.astype(BF16)

    key1.relay()
    val1.relay()
    up_a.relay1()
    up_b.start()

    over_k.wait_recv()
    over_v.wait_recv()
    edge = (y == 3).astype(F32)
    for src, over, staged in ((k_in, zk, sk), (v_in, zv, sv)):
        staged[...] = (
            over[...].astype(F32) * edge + src[...].astype(F32) * (1.0 - edge)
        ).astype(BF16)
    next_k = send(sk, kprev, ys[1])
    next_v = send(sv, vprev, ys[1])

    gate_a.relay1()
    down_a.relay1()
    key1.finish()
    key2a.start()
    key2b.start()
    up_a.finish1()
    up_a.turn()
    up_b.relay1()
    val1.finish()
    val2a.start()
    val2b.start()

    def spread_z(buf, lanes):
        return [
            send(buf.at[0, :, lanes], buf.at[3, :, lanes], zs[1]),
            send(buf.at[0, :, lanes], buf.at[1, :, lanes], zs[-1]),
        ]

    def onward(buf, copies, lanes):
        copies[0].wait_recv()
        a = send(buf.at[3, pl.ds(0, 64), lanes], buf.at[2, pl.ds(0, 64), lanes], zs[1])
        copies[1].wait_recv()
        b = send(buf.at[1, pl.ds(64, 64), lanes], buf.at[2, pl.ds(64, 64), lanes], zs[-1])
        return [a, b]

    res_lanes = [pl.ds(512 * n, 512) for n in range(4)]
    head_lanes = [pl.ds(256 * n, 256) for n in range(4)]
    local_res.wait()
    res_copies = [spread_z(res, res_lanes[0])]
    spread(k_in, ks, 128)
    spread(v_in, vs, 128)
    key2a.relay()
    up_b.finish1()
    up_b.turn()
    gate_a.finish1()
    key2b.relay()
    res_copies += [spread_z(res, lanes) for lanes in res_lanes[1:]]
    val2a.relay()
    up_a.relay2()
    val2b.relay()
    gate_b.start()
    down_b.start()
    next_k.wait_recv()
    next_v.wait_recv()
    spread(kprev, ks, 0)
    spread(vprev, vs, 0)
    key2a.finish()
    val2a.finish()

    bias4 = jnp.concatenate([bias] * 4, axis=0)
    in_group4 = jnp.concatenate([in_group] * 4, axis=0)

    def head(h):
        lanes = slice(256 * h, 256 * h + 256)
        block = q_in[:, lanes].astype(F32) * 0.125
        rows = [part * in_group for b in (0, 1) for part in twice(block[:, 128 * b:128 * b + 128])]
        qx = jnp.concatenate(rows, axis=0).astype(BF16)
        keys = kbuf[:, :, h].reshape(1024, 256)
        contract = (((1,), (1,)), ((), ()))
        s1 = lax.dot_general(qx, keys, contract, preferred_element_type=F32)
        s2 = lax.dot_general(qx, ks[h], contract, preferred_element_type=F32) + bias4
        peak = jnp.maximum(
            jnp.max(s1, axis=1, keepdims=True), jnp.max(s2, axis=1, keepdims=True)
        )
        p1, p2 = jnp.exp(s1 - peak), jnp.exp(s2 - peak)
        total = jnp.sum(p1, axis=1, keepdims=True) + jnp.sum(p2, axis=1, keepdims=True)
        o = jnp.dot(p1.astype(BF16), vbuf[:, :, h].reshape(1024, 256), preferred_element_type=F32)
        o = o + jnp.dot(p2.astype(BF16), vs[h], preferred_element_type=F32)
        o = o * in_group4
        o = o[:, :128] + o[:, 128:]
        o = (o + pltpu.roll(o, 64, 1)) * (1.0 / total)
        left, right = jnp.where(low, o[0:128], o[128:256]), jnp.where(low, o[256:384], o[384:512])
        attn[0, :, lanes] = jnp.concatenate([left, right], axis=1).astype(BF16)

    head(0)
    attn_copies = [spread_z(attn, head_lanes[0])]
    key2b.finish()
    val2b.finish()
    head(1)
    attn_copies.append(spread_z(attn, head_lanes[1]))
    up_b.relay2()
    arriving = [onward(res, res_copies[0], res_lanes[0])]
    arriving.append(onward(res, res_copies[1], res_lanes[1]))
    gate_b.relay1()
    head(2)
    attn_copies.append(spread_z(attn, head_lanes[2]))
    down_b.relay1()
    gate_a.turn()
    arriving.append(onward(attn, attn_copies[0], head_lanes[0]))
    gate_b.finish1()
    gate_b.turn()
    head(3)
    attn_copies.append(spread_z(attn, head_lanes[3]))
    arriving.append(onward(attn, attn_copies[1], head_lanes[1]))
    arriving.append(onward(res, res_copies[2], res_lanes[2]))
    arriving.append(onward(res, res_copies[3], res_lanes[3]))
    arriving.append(onward(attn, attn_copies[2], head_lanes[2]))
    up_a.finish2()
    down_a.finish1()
    last = onward(attn, attn_copies[3], head_lanes[3])
    up_b.finish2()
    local_out.wait()
    for copies in arriving:
        for copy in copies:
            copy.wait_recv()

    down_b.finish1()

    def project_first(n, carry):
        lanes = pl.ds(pl.multiple_of(n * 256, 256), 256)
        upv[n] = res[:, :, lanes].reshape(512, 256).astype(F32) + jnp.dot(
            attn[:, :, 0:768].reshape(512, 768), owb[0:768, lanes], preferred_element_type=F32
        )

        @pl.when(n == 4)
        def _():
            gate_a.relay2()
            down_a.turn()

        @pl.when(n == 7)
        def _():
            gate_b.relay2()
            down_b.turn()

        return carry

    lax.fori_loop(0, 8, project_first, 0)
    for copy in last:
        copy.wait_recv()

    def project(n, square):
        lanes = pl.ds(pl.multiple_of(n * 256, 256), 256)
        part = upv[n] + jnp.dot(
            attn[:, :, 768:1024].reshape(512, 256), owb[768:1024, lanes], preferred_element_type=F32
        )
        upv[n] = part
        hid[:, lanes] = part[0:128]
        return square + jnp.sum(part * part, axis=1, keepdims=True)

    square = lax.fori_loop(0, 8, project, jnp.zeros((512, 1), F32))
    scale = lax.rsqrt(square * (1.0 / 2048) + EPSILON)

    def normalize(n, carry):
        lanes = pl.ds(pl.multiple_of(n * 256, 256), 256)
        xn[:, lanes] = (upv[n] * scale * gain_in[:, lanes]).astype(BF16)
        return carry

    lax.fori_loop(0, 8, normalize, 0)
    up_a.ready()
    up_b.ready()

    def unit_columns(i):
        return i // 2, pl.ds(pl.multiple_of(lax.rem(i, 2) * 256, 256), 256)

    def up_units(i, carry):
        block, cols = unit_columns(i)
        upv[i] = jnp.dot(
            xn[...], wu[block, :, :, :, cols].reshape(2048, 256), preferred_element_type=F32
        )

        @pl.when(i == 3)
        def _():
            gate_a.finish2()

        @pl.when(i == 5)
        def _():
            gate_b.finish2()

        return carry

    lax.fori_loop(0, 8, up_units, 0)
    gate_a.ready()
    gate_b.ready()

    def gate_units(i, carry):
        block, cols = unit_columns(i)
        g = jnp.dot(
            xn[...], wg[block, :, :, :, cols].reshape(2048, 256), preferred_element_type=F32
        )
        act[:, pl.ds(pl.multiple_of(i * 256, 256), 256)] = (
            g / (1.0 + jnp.exp(-g)) * upv[i]
        ).astype(BF16)

        @pl.when(i == 4)
        def _():
            down_a.relay2()

        return carry

    lax.fori_loop(0, 8, gate_units, 0)
    down_b.ready(1)

    half0, half1 = pl.ds(0, 64), pl.ds(64, 64)
    first_hop = counter[0]
    counter[0] += 32

    def place(k):
        kind = 1 - lax.rem((k + 1) // 4, 2)
        i = lax.rem(x + k + k // 2, 4) * kind + (k - 3) * (1 - kind)
        return kind, i, kind * 4 + i

    def hop_copies(k):
        n = place(k)[2]
        return [
            pltpu.make_async_remote_copy(
                src_ref=src, dst_ref=dst, send_sem=ssem.at[first_hop + j * 8 + k],
                recv_sem=rsem.at[first_hop + j * 8 + k], device_id=device, device_id_type=MESH,
            )
            for j, (src, dst, device) in enumerate((
                (far.at[n, half0], hop.at[0, n], zs[1]),
                (far.at[n, half1], hop.at[1, n], zs[-1]),
                (near.at[0, n], back.at[0, n], zs[1]),
                (near.at[1, n], back.at[1, n], zs[-1]),
            ))
        ]

    def pass_on(k):
        n = place(k)[2]
        copies = hop_copies(k)
        copies[0].wait_recv()
        near[0, n, 0:64] = (ends[0, n, 0:64] + hop[0, n].astype(F32)).astype(BF16)
        near[0, n, 64:128] = ends[0, n, 64:128].astype(BF16)
        copies[2].start()
        copies[1].wait_recv()
        near[1, n, 0:64] = ends[1, n, 0:64].astype(BF16)
        near[1, n, 64:128] = (ends[1, n, 64:128] + hop[1, n].astype(F32)).astype(BF16)
        copies[3].start()

    def down_step(k, carry):
        @pl.when(k == 1)
        def _():
            down_b.relay2()
            pass_on(0)
            down_b.ready(2)

        @pl.when(k == 2)
        def _():
            down_a.finish2()

        @pl.when(k == 3)
        def _():
            down_a.ready()

        @pl.when(k == 4)
        def _():
            down_b.finish2()

        @pl.when(k == 7)
        def _():
            down_b.ready()

        @pl.when(k < 8)
        def _():
            kind, i, n = place(k)
            weight = jnp.concatenate(
                [wd[kind, 0, i].reshape(2048, 128), wd[kind, 1, i].reshape(2048, 128)], axis=1
            )
            part = jnp.dot(act[...], weight, preferred_element_type=F32)
            far[n] = part[256:384].astype(BF16)
            copies = hop_copies(k)
            copies[0].start()
            copies[1].start()
            acc[n] = part[0:128]
            ends[0, n] = part[128:256]
            ends[1, n] = part[384:512]

        @pl.when(k > 2)
        def _():
            pass_on(k - 2)

        return carry

    lax.fori_loop(0, 10, down_step, 0)

    def collect(k, carry):
        copies = hop_copies(k)
        copies[2].wait_recv()
        copies[3].wait_recv()
        kind, i, n = place(k)
        total = acc[n] + back[0, n].astype(F32) + back[1, n].astype(F32)
        for cc in range(2):
            lanes = pl.ds(pl.multiple_of(512 * i + 256 * cc + 128 * kind, 128), 128)
            out[:, lanes] = (hid[:, lanes] + total[:, 128 * cc:128 * cc + 128]).astype(BF16)
        return carry

    lax.fori_loop(0, 8, collect, 0)
    for k in range(8):
        started.extend(hop_copies(k))

    for copy in started:
        copy.wait_send()
    assert counter[0] == N_SEM, counter[0]


def shards(
    residual, queries, keys, values, prefix_keys, cached_prefix_values, out_weight, norm_gain,
    w_gate, w_up, w_down, suffix_lengths, request_group, placement_order,
):
    vmem = pl.BlockSpec(memory_space=pltpu.VMEM)
    anywhere = pl.BlockSpec(memory_space=pl.ANY)
    return pl.pallas_call(
        kernel,
        out_shape=jax.ShapeDtypeStruct((128, 2048), BF16),
        in_specs=[
            anywhere, vmem, vmem, vmem, vmem, vmem, anywhere, vmem,
            anywhere, anywhere, anywhere, vmem, vmem, vmem,
        ],
        out_specs=vmem,
        scratch_shapes=[
            pltpu.VMEM((4, 4, 4, 64, 256), BF16),
            pltpu.VMEM((4, 4, 4, 64, 256), BF16),
            pltpu.VMEM((128, 256), BF16),
            pltpu.VMEM((128, 256), BF16),
            pltpu.VMEM((128, 256), BF16),
            pltpu.VMEM((128, 256), BF16),
            pltpu.VMEM((128, 256), BF16),
            pltpu.VMEM((128, 256), BF16),
            pltpu.VMEM((4, 256, 256), BF16),
            pltpu.VMEM((4, 256, 256), BF16),
            pltpu.VMEM((4, 128, 1024), BF16),
            pltpu.VMEM((1024, 2048), BF16),
            pltpu.VMEM((4, 128, 2048), BF16),
            pltpu.VMEM((128, 2048), F32),
            pltpu.VMEM((512, 2048), BF16),
            pltpu.VMEM((4, 4, 2, 256, 512), BF16),
            pltpu.VMEM((4, 4, 2, 256, 512), BF16),
            pltpu.VMEM((2, 2, 4, 4, 512, 128), BF16),
            pltpu.VMEM((8, 512, 256), F32),
            pltpu.VMEM((512, 2048), BF16),
            pltpu.VMEM((8, 128, 256), F32),
            pltpu.VMEM((2, 8, 128, 256), F32),
            pltpu.VMEM((8, 128, 256), BF16),
            pltpu.VMEM((2, 8, 64, 256), BF16),
            pltpu.VMEM((2, 8, 128, 256), BF16),
            pltpu.VMEM((2, 8, 128, 256), BF16),
            pltpu.SemaphoreType.DMA((N_SEM,)),
            pltpu.SemaphoreType.DMA((N_SEM,)),
            pltpu.SemaphoreType.DMA((6,)),
        ],
        compiler_params=pltpu.CompilerParams(
            collective_id=0, has_side_effects=True, vmem_limit_bytes=63 << 20
        ),
    )(
        residual, queries, keys, values, prefix_keys, cached_prefix_values, out_weight,
        norm_gain.reshape(1, -1), w_gate, w_up, w_down,
        suffix_lengths, request_group, placement_order,
    )


def solution(mesh):
    placed = (
        P(("grp", "dev"), None),
        P(("grp", "dev"), None),
        P(("grp", "dev"), None),
        P(("grp", "dev"), None),
        P("grp", "dev", None),
        P("grp", "dev", None),
        P(),
        P(),
        P("grp", "dev"),
        P("grp", "dev"),
        P("dev", "grp"),
        P("grp", None),
        P("grp", None),
        P("grp", None),
    )
    return jax.shard_map(
        shards, mesh=mesh, in_specs=placed, out_specs=P(("grp", "dev"), None), check_vma=False
    )
```
